512 devices in a mesh: vocab: 128 (over y_lo, z, x, core), seq: 4 (over y_hi).
Axes of the slice: x: 4, y: 8 (y_hi: 4, y_lo: 2; y = y_hi * 2 + y_lo), z: 8, core: 2. Of those that a mesh axis runs over, the one named last changes fastest.
Arguments:
- latent_vector: bfloat16 [512, 7168], P('vocab', 'seq'), may hold values from -400 to 400
- unembedding_matrix: bfloat16 [7168, 131072], P('seq', 'vocab'), may hold values from -0.0625 to 0.0625
- occurrence_tally: int32 [512, 131072], P(('seq', 'vocab')), may hold values from 0 to 2
- additive_offset_table: bfloat16 [512, 131072], P(('seq', 'vocab')), may hold values from 0 to 0.5
- recurrence_charge: float32 [512], P(('seq', 'vocab')), may hold values from 0.05 to 0.5
- appearance_charge: float32 [512], P(('seq', 'vocab')), may hold values from 0.6 to 1.5
- recurrence_divisor: float32 [512], P('seq'), may hold values from 1.05 to 1.6
- softening_divisor: float32 [512], P('seq'), may hold values from 0.5 to 1.5
- nucleus_share_limit: float32 [512], P('seq'), may hold values from 0.5 to 0.95
Outputs:
- penalized_logits: bfloat16 [512, 131072], P('seq', 'vocab')
- cutoff: float32 [512], P('seq')
The draws below stay inside these ranges and needn't reach their ends.
Inputs may be any that keep to these rules, and one draw needn't show every extreme that they name: `appearance_charge`: each sequence's presence penalty exceeds every entry of its token bias.
All inputs are finite; a program needn't handle non-finite values.
Results may differ from the reference program's by a relative error of at most 0.0047.
Values may be sent and summed in bfloat16 or wider, within the bound.
A program may use at most 64 MiB of HBM per device.

```python
import math
import jax
import jax.numpy as jnp
from jax import lax

D = 7168
STEPS = 9
STRAND_COUNT = 512
VOCAB = 131072


def draw_latent_vector(key, part):
    normal_part = jax.random.normal(jax.random.fold_in(key, 11), (STRAND_COUNT, D), jnp.float32)
    return jnp.clip(normal_part, -400.0, 400.0).astype(jnp.bfloat16)


def set_ends(result, own_key, least, high):
    longest = result.shape.index(max(result.shape))
    spots = []
    for shift in (0, 1):
        where = [jax.random.randint(jax.random.fold_in(own_key, axis), (), 0, length) for axis, length in enumerate(result.shape)]
        where[longest] = (where[longest] + shift) % result.shape[longest]
        spots.append(tuple(where))
    return result.at[spots[0]].set(least).at[spots[1]].set(high)


def levels(rng, shape, cuts, low, largest):
    def one(dim, parts):
        draws = jax.random.uniform(jax.random.fold_in(jax.random.fold_in(rng, 6), dim), (parts,), jnp.float32, low / len(cuts), largest / len(cuts))
        return jnp.repeat(jnp.exp(draws), shape[dim] // parts).reshape((-1,) + (1,) * (len(shape) - dim - 1))

    factor_of = one(*cuts[0])
    for cut in cuts[1:]:
        factor_of = factor_of * one(*cut)
    return factor_of


def noise(rng, shape, deviation, reach, cuts=(), held_as=jnp.bfloat16):
    gain = levels(rng, shape, cuts, -0.22, 0.18) if cuts else 1.0
    array = jax.random.normal(rng, shape, jnp.float32) * deviation * gain
    return jnp.minimum(jnp.maximum(array, -reach), reach).astype(held_as)


def setup_inputs(seed: int = 0) -> dict:
    streams_of = jax.random.split(jax.random.key(seed), 10)
    latent_vector = draw_latent_vector(jax.random.fold_in(streams_of[9], 71), 0)
    unembedding_matrix = noise(streams_of[1], (D, VOCAB), D ** -0.5, 0.0625, ((0, 4), (1, 128)))
    occurrence_tally = set_ends(jax.random.randint(streams_of[2], (STRAND_COUNT, VOCAB), 0, 3), jax.random.fold_in(streams_of[2], 1), 0, 2).astype(jnp.int32)
    additive_offset_table = jnp.clip(0.5 * jax.random.uniform(streams_of[3], (STRAND_COUNT, VOCAB), jnp.float32) ** levels(streams_of[3], (STRAND_COUNT, VOCAB), ((0, 512),), -0.2, 0.2), 0.0, 0.5).astype(jnp.bfloat16)
    recurrence_charge = jnp.clip(jnp.exp(math.log(0.5) - 2.3025851 * jax.random.uniform(streams_of[4], (STRAND_COUNT,), jnp.float32) ** levels(streams_of[4], (STRAND_COUNT,), ((0, 512),), -0.2, 0.2)), 0.05, 0.5)
    appearance_charge = jnp.clip(jnp.exp(math.log(1.5) - 0.9162907 * jax.random.uniform(streams_of[5], (STRAND_COUNT,), jnp.float32) ** levels(streams_of[5], (STRAND_COUNT,), ((0, 512),), -0.2, 0.2)), 0.6, 1.5)
    recurrence_divisor = jnp.clip(jnp.exp(math.log(1.6) - 0.42121353 * jax.random.uniform(streams_of[6], (STRAND_COUNT,), jnp.float32) ** levels(streams_of[6], (STRAND_COUNT,), ((0, 4),), -0.2, 0.2)), 1.05, 1.6)
    softening_divisor = jnp.clip(jnp.exp(math.log(1.5) - 1.0986123 * jax.random.uniform(streams_of[7], (STRAND_COUNT,), jnp.float32) ** levels(streams_of[7], (STRAND_COUNT,), ((0, 4),), -0.2, 0.2)), 0.5, 1.5)
    nucleus_share_limit = jnp.clip(0.5 + 0.45 * jax.random.uniform(streams_of[8], (STRAND_COUNT,), jnp.float32) ** levels(streams_of[8], (STRAND_COUNT,), ((0, 4),), -0.2, 0.2), 0.5, 0.95)
    return dict(latent_vector=latent_vector, unembedding_matrix=unembedding_matrix, occurrence_tally=occurrence_tally, additive_offset_table=additive_offset_table, recurrence_charge=recurrence_charge, appearance_charge=appearance_charge, recurrence_divisor=recurrence_divisor, softening_divisor=softening_divisor, nucleus_share_limit=nucleus_share_limit)


cutoff_span = 32.0


def reference(latent_vector, unembedding_matrix, occurrence_tally, additive_offset_table, recurrence_charge, appearance_charge, recurrence_divisor, softening_divisor, nucleus_share_limit):
    logits = jnp.dot(latent_vector, unembedding_matrix, preferred_element_type=jnp.float32)
    count_float = occurrence_tally.astype(jnp.float32)
    seen_mask = occurrence_tally > 0
    offset = (additive_offset_table.astype(jnp.float32) - recurrence_charge[:, None] * count_float
              - appearance_charge[:, None] * seen_mask.astype(jnp.float32)).astype(jnp.bfloat16)
    factor = recurrence_divisor[:, None]
    discouraged_scores = jnp.where(seen_mask, jnp.where(logits > 0, logits / factor, logits * factor), logits) + offset.astype(jnp.float32)
    softened_scores = discouraged_scores / softening_divisor[:, None]
    largest_score = jnp.max(softened_scores, axis=1)
    exponential_values = jnp.exp(softened_scores - largest_score[:, None])
    row_total = jnp.sum(exponential_values, axis=1)
    target = nucleus_share_limit * row_total

    def bisect_step(turn_index, bounds):
        lower_end, upper_end = bounds
        middle = (lower_end + upper_end) * 0.5
        threshold_candidates = largest_score - cutoff_span * middle
        cumulative_shares = jnp.sum(jnp.where(softened_scores >= threshold_candidates[:, None], exponential_values, 0.0), axis=1)
        below_mask = cumulative_shares < target
        return jnp.where(below_mask, middle, lower_end), jnp.where(below_mask, upper_end, middle)

    start_bounds = (jnp.zeros_like(largest_score), jnp.ones_like(largest_score))
    lower_end, upper_end = lax.fori_loop(0, STEPS, bisect_step, start_bounds)
    return discouraged_scores.astype(jnp.bfloat16), largest_score - cutoff_span * upper_end
```

```python
import functools

import jax
import jax.numpy as jnp
from jax import lax
from jax.experimental import pallas as pl
from jax.experimental.pallas import tpu as pltpu
from jax.sharding import Mesh
from jax.sharding import PartitionSpec as P

VOCAB = ("vocab_0", "vocab_1", "vocab_2", "vocab_3")
SEQ_VOCAB = ("seq", "vocab_0", "vocab_1", "vocab_2", "vocab_3")
MESH = pl.DeviceIdType.MESH
NEAR = 16
FAR = 8
LEVELS = (31, 15)
SPAN = 32.0


def sent_to_all(array, axis):
    count = lax.axis_size(axis)
    return lax.all_to_all(
        jnp.broadcast_to(array[None], (count, *array.shape)), axis, 0, 0, tiled=True
    )


def gather_axes(array, axes, dim):
    far, near = axes
    first = sent_to_all(array, far)
    tiles = jnp.swapaxes(sent_to_all(first, near), 0, 1)
    tiles = tiles.reshape(-1, *array.shape)
    return tiles.reshape(-1, array.shape[1])


def sum_at_owner(array, axis):
    count = lax.axis_size(axis)
    tiles = array.reshape(count, array.shape[0] // count, array.shape[1])
    arrived = lax.all_to_all(tiles, axis, split_axis=0, concat_axis=0, tiled=True)
    return arrived.sum(axis=0)


def near_index():
    return (
        lax.axis_index("vocab_0") * 8
        + lax.axis_index("vocab_2") * 2
        + lax.axis_index("vocab_3")
    )


def near_peer(index):
    return {
        "vocab_0": index // 8,
        "vocab_2": lax.rem(index // 2, 4),
        "vocab_3": lax.rem(index, 2),
    }


def far_peer(index):
    return {"vocab_1": index}


def exchange(held, me, count, peer, send_sem, recv_sem):
    copies = []
    for step in range(1, count):
        there = lax.rem(me + step, count)
        copy = pltpu.make_async_remote_copy(
            src_ref=held.at[me],
            dst_ref=held.at[me],
            send_sem=send_sem.at[step],
            recv_sem=recv_sem.at[step],
            device_id=peer(there),
            device_id_type=MESH,
        )
        copy.start()
        copies.append(copy)
    for step in range(1, count):
        source = lax.rem(me + count - step, count)
        pltpu.make_async_remote_copy(
            src_ref=held.at[me],
            dst_ref=held.at[source],
            send_sem=send_sem.at[step],
            recv_sem=recv_sem.at[step],
            device_id=peer(source),
            device_id_type=MESH,
        ).wait_recv()
    return copies


def reduced(values, near, far, sems, combine):
    here, there = near_index(), lax.axis_index("vocab_1")
    near[here] = values
    sent = exchange(near, here, NEAR, near_peer, sems[0], sems[1])
    part = near[0]
    for k in range(1, NEAR):
        part = combine(part, near[k])
    far[there] = part
    sent += exchange(far, there, FAR, far_peer, sems[2], sems[3])
    whole = far[0]
    for k in range(1, FAR):
        whole = combine(whole, far[k])
    return whole, sent


def masses(scores, weights, limits):
    rows = []
    chunks = scores.shape[0] // 8
    for start in range(0, len(limits), 8):
        group = [jnp.broadcast_to(t, (8, 128)) for t in limits[start : start + 8]]

        def add(k, sums, group=group):
            at = pl.ds(pl.multiple_of(k * 8, 8), 8)
            s, w = scores[at, :], weights[at, :]
            return tuple(a + jnp.where(s >= t, w, 0.0) for a, t in zip(sums, group))

        zero = jnp.zeros((8, 128), jnp.float32)
        sums = lax.fori_loop(0, chunks, add, (zero,) * len(group), unroll=8)
        rows += [jnp.sum(a, axis=0, keepdims=True) for a in sums]
    return rows


def tail_kernel(
    logits,
    offset,
    divisor,
    softening,
    share,
    out,
    cutoff,
    scores,
    weights,
    near_a,
    far_a,
    near_b,
    far_b,
    near_c,
    far_c,
    sem_near_send,
    sem_near_recv,
    sem_far_send,
    sem_far_recv,
):
    barrier = pltpu.get_barrier_semaphore()
    here, there = near_index(), lax.axis_index("vocab_1")
    for step in range(1, NEAR):
        pl.semaphore_signal(
            barrier, inc=1, device_id=near_peer(lax.rem(here + step, NEAR)), device_id_type=MESH
        )
    for step in range(1, FAR):
        pl.semaphore_signal(
            barrier, inc=1, device_id=far_peer(lax.rem(there + step, FAR)), device_id_type=MESH
        )

    inverse = 1.0 / divisor[...]
    cooler = 1.0 / softening[...]
    highest = None
    for k in range(logits.shape[1] // 128):
        at = pl.ds(k * 128, 128)
        raw, shift = logits[:, at], offset[:, at].astype(jnp.float32)
        scaled = jnp.where(raw > 0, raw * inverse, raw * divisor[...])
        changed = jnp.where(shift < 0, scaled, raw) + shift
        out[:, at] = changed.astype(jnp.bfloat16)
        turned = (changed * cooler).T
        scores[at, :] = turned
        most = jnp.max(turned, axis=0, keepdims=True)
        highest = most if highest is None else jnp.maximum(highest, most)
    pl.semaphore_wait(barrier, NEAR + FAR - 2)

    def sems(turn):
        return (
            sem_near_send.at[turn],
            sem_near_recv.at[turn],
            sem_far_send.at[turn],
            sem_far_recv.at[turn],
        )

    largest, sent = reduced(highest, near_a, far_a, sems(0), jnp.maximum)
    total = jnp.zeros((8, 128), jnp.float32)
    chunk = 64
    for k in range(scores.shape[0] // chunk):
        at = pl.ds(k * chunk, chunk)
        terms = jnp.exp(scores[at, :] - largest)
        weights[at, :] = terms
        total = total + jnp.sum(terms.reshape(chunk // 8, 8, 128), axis=0)

    first = [largest - (SPAN / (LEVELS[0] + 1)) * (k + 1) for k in range(LEVELS[0])]
    rows = [jnp.sum(total, axis=0, keepdims=True)] + masses(scores, weights, first)
    sums, more = reduced(jnp.concatenate(rows), near_b, far_b, sems(1), jnp.add)
    sent += more
    target = share[...] * sums[0:1]
    lower = jnp.sum(
        jnp.where(sums[1:] < target, 1.0, 0.0), axis=0, keepdims=True
    ) * (LEVELS[1] + 1)

    unit = SPAN / ((LEVELS[0] + 1) * (LEVELS[1] + 1))
    second = [largest - unit * (lower + (k + 1)) for k in range(LEVELS[1])]
    rows = masses(scores, weights, second)
    rows.append(rows[-1])
    sums, more = reduced(jnp.concatenate(rows), near_c, far_c, sems(2), jnp.add)
    sent += more
    below = jnp.where(sums[: LEVELS[1]] < target, 1.0, 0.0)
    lower = lower + jnp.sum(below, axis=0, keepdims=True)
    cutoff[...] = largest - unit * (lower + 1.0)
    for copy in sent:
        copy.wait_send()


def tail(logits, offset, divisor, softening, share):
    rows, columns = logits.shape
    vmem = pl.BlockSpec(memory_space=pltpu.VMEM)

    def held(count, depth):
        return pltpu.VMEM((count, depth, 128), jnp.float32)

    return pl.pallas_call(
        tail_kernel,
        out_shape=(
            jax.ShapeDtypeStruct((rows, columns), jnp.bfloat16),
            jax.ShapeDtypeStruct((1, rows), jnp.float32),
        ),
        in_specs=[vmem] * 5,
        out_specs=(vmem, vmem),
        scratch_shapes=[
            pltpu.VMEM((columns, rows), jnp.float32),
            pltpu.VMEM((columns, rows), jnp.float32),
            held(NEAR, 1),
            held(FAR, 1),
            held(NEAR, LEVELS[0] + 1),
            held(FAR, LEVELS[0] + 1),
            held(NEAR, LEVELS[1] + 1),
            held(FAR, LEVELS[1] + 1),
            pltpu.SemaphoreType.DMA((3, NEAR)),
            pltpu.SemaphoreType.DMA((3, NEAR)),
            pltpu.SemaphoreType.DMA((3, FAR)),
            pltpu.SemaphoreType.DMA((3, FAR)),
        ],
        compiler_params=pltpu.CompilerParams(collective_id=1, has_side_effects=True),
        name="tail",
    )(logits, offset, divisor[:, None], softening[:, None], share[None, :])


def per_device(
    latent_vector,
    unembedding_matrix,
    occurrence_tally,
    additive_offset_table,
    recurrence_charge,
    appearance_charge,
    recurrence_divisor,
    softening_divisor,
    nucleus_share_limit,
):
    count_float = occurrence_tally.astype(jnp.float32)
    offset = (
        additive_offset_table.astype(jnp.float32)
        - recurrence_charge[:, None] * count_float
        - appearance_charge[:, None] * (occurrence_tally > 0).astype(jnp.float32)
    ).astype(jnp.bfloat16)
    relaid = lax.all_to_all(offset, VOCAB, split_axis=1, concat_axis=0, tiled=True)
    partial_logits = jnp.dot(
        gather_axes(latent_vector, (("vocab_0", "vocab_1", "vocab_2"), "vocab_3"), 0),
        unembedding_matrix,
        preferred_element_type=jnp.float32,
    )
    logits = sum_at_owner(partial_logits, "seq")
    out, cutoff = tail(
        logits, relaid, recurrence_divisor, softening_divisor, nucleus_share_limit
    )
    return out, cutoff.reshape(-1)


def solution(mesh):
    split = Mesh(
        mesh.devices.reshape(2, 8, 4, 2, mesh.shape["seq"]),
        ("vocab_0", "vocab_1", "vocab_2", "vocab_3", "seq"),
    )
    placed = (
        P(VOCAB, "seq"),
        P("seq", VOCAB),
        P(SEQ_VOCAB, None),
        P(SEQ_VOCAB, None),
        P(SEQ_VOCAB),
        P(SEQ_VOCAB),
        P("seq"),
        P("seq"),
        P("seq"),
    )
    return jax.shard_map(
        per_device,
        mesh=split,
        in_specs=placed,
        out_specs=(P("seq", VOCAB), P("seq")),
        check_vma=False,
    )
```

```python
import itertools

import jax
import jax.numpy as jnp
from jax import lax
from jax.experimental import pallas as pl
from jax.experimental.pallas import tpu as pltpu
from jax.sharding import Mesh
from jax.sharding import PartitionSpec as P

VOCAB = ("vocab_0", "vocab_1", "vocab_2", "vocab_3")
SEQ_VOCAB = ("seq", "vocab_0", "vocab_1", "vocab_2", "vocab_3")
MESH = pl.DeviceIdType.MESH
NEAR = 16
FAR = 8
LEVELS = (31, 15)
SPAN = 32.0
PARTS = 4
COPIES = 96


def near_index():
    return (
        lax.axis_index("vocab_0") * 8
        + lax.axis_index("vocab_2") * 2
        + lax.axis_index("vocab_3")
    )


def near_peer(index):
    return {
        "vocab_0": index // 8,
        "vocab_2": lax.rem(index // 2, 4),
        "vocab_3": lax.rem(index, 2),
    }


def far_peer(index):
    return {"vocab_1": index}


def exchange(held, me, count, peer, send_sem, recv_sem):
    copies = []
    for step in range(1, count):
        there = lax.rem(me + step, count)
        copy = pltpu.make_async_remote_copy(
            src_ref=held.at[me],
            dst_ref=held.at[me],
            send_sem=send_sem.at[step],
            recv_sem=recv_sem.at[step],
            device_id=peer(there),
            device_id_type=MESH,
        )
        copy.start()
        copies.append(copy)
    for step in range(1, count):
        source = lax.rem(me + count - step, count)
        pltpu.make_async_remote_copy(
            src_ref=held.at[me],
            dst_ref=held.at[source],
            send_sem=send_sem.at[step],
            recv_sem=recv_sem.at[step],
            device_id=peer(source),
            device_id_type=MESH,
        ).wait_recv()
    return copies


def reduced(values, near, far, sems, combine):
    here, there = near_index(), lax.axis_index("vocab_1")
    near[here] = values
    sent = exchange(near, here, NEAR, near_peer, sems[0], sems[1])
    part = near[0]
    for k in range(1, NEAR):
        part = combine(part, near[k])
    far[there] = part
    sent += exchange(far, there, FAR, far_peer, sems[2], sems[3])
    whole = far[0]
    for k in range(1, FAR):
        whole = combine(whole, far[k])
    return whole, sent


def masses(scores, weights, limits):
    rows = []
    chunks = scores.shape[0] // 8
    for start in range(0, len(limits), 8):
        group = [jnp.broadcast_to(t, (8, 128)) for t in limits[start : start + 8]]

        def add(k, sums, group=group):
            at = pl.ds(pl.multiple_of(k * 8, 8), 8)
            s, w = scores[at, :], weights[at, :]
            return tuple(a + jnp.where(s >= t, w, 0.0) for a, t in zip(sums, group))

        zero = jnp.zeros((8, 128), jnp.float32)
        sums = lax.fori_loop(0, chunks, add, (zero,) * len(group), unroll=8)
        rows += [jnp.sum(a, axis=0, keepdims=True) for a in sums]
    return rows


def step_kernel(
    latent,
    weights_hbm,
    offset,
    divisor,
    softening,
    share,
    out,
    cutoff,
    weights,
    few,
    hidden,
    partial,
    relay_in,
    direct_in,
    final_in,
    far_offset,
    near_offset,
    scores,
    terms,
    near_a,
    far_a,
    near_b,
    far_b,
    near_c,
    far_c,
    send_sem,
    recv_sem,
    local_sem,
    sem_near_send,
    sem_near_recv,
    sem_far_send,
    sem_far_recv,
):
    y, z = lax.axis_index("vocab_0"), lax.axis_index("vocab_1")
    x, core = lax.axis_index("vocab_2"), lax.axis_index("vocab_3")
    seq = lax.axis_index("seq")
    here, pair = near_index(), x * 2 + core
    half = latent.shape[1] // 2
    rows, columns = out.shape
    mid, wide = rows // 2, columns // PARTS

    load = pltpu.make_async_copy(weights_hbm, weights, local_sem.at[0])
    load.start()
    barrier = pltpu.get_barrier_semaphore()

    def greet(peer):
        pl.semaphore_signal(barrier, inc=1, device_id=peer, device_id_type=MESH)

    for step in range(1, NEAR):
        greet(near_peer(lax.rem(here + step, NEAR)))
    for step in range(1, FAR):
        greet(far_peer(lax.rem(z + step, FAR)))
    after, before = {"seq": lax.rem(seq + 1, 4)}, {"seq": lax.rem(seq + 3, 4)}
    greet(after)
    greet(before)

    numbers = itertools.count()
    sent = []

    def describe(number, source, target, peer):
        return pltpu.make_async_remote_copy(
            src_ref=source,
            dst_ref=target,
            send_sem=send_sem.at[number],
            recv_sem=recv_sem.at[number],
            device_id=peer,
            device_id_type=MESH,
        )

    def send(source, target, peer):
        number = next(numbers)
        copy = describe(number, source, target, peer)
        copy.start()
        sent.append(copy)
        return number

    def arrive(number, landing, peer):
        describe(number, landing, landing, peer).wait_recv()

    def my_half(which):
        return pl.ds(pl.multiple_of(which * half, 128), half)

    few[pair] = latent[:, my_half(core)]
    pl.semaphore_wait(barrier, NEAR + FAR)

    def pair_peer(index):
        return {"vocab_2": index // 2, "vocab_3": lax.rem(index, 2)}

    order = [4, 5, 3, 1, 2, 6, 7]
    swaps = {}
    for step in order:
        there = lax.rem(pair + step, 8)
        swaps[step] = send(
            latent.at[:, my_half(lax.rem(there, 2))], few.at[pair], pair_peer(there)
        )
    for step in order:
        source = lax.rem(pair + 8 - step, 8)
        arrive(swaps[step], few.at[source], pair_peer(source))
    joined = jnp.concatenate([few[k].astype(jnp.float32) for k in range(8)])

    def block(which_y, which_z):
        at = pl.multiple_of((which_y * FAR + which_z) * 32, 32)
        return hidden.at[core, pl.ds(at, 32)]

    hidden[core, pl.ds(pl.multiple_of((y * FAR + z) * 32, 32), 32)] = joined.astype(
        jnp.bfloat16
    )

    other_core, other_y = {"vocab_3": 1 - core}, {"vocab_0": 1 - y}
    up, down = {"vocab_1": lax.rem(z + 1, FAR)}, {"vocab_1": lax.rem(z + 7, FAR)}
    shares = []

    def to_core(which_y, which_z):
        number = send(block(which_y, which_z), block(which_y, which_z), other_core)
        at = pl.multiple_of((which_y * FAR + which_z) * 32, 32)
        shares.append((number, hidden.at[1 - core, pl.ds(at, 32)]))

    def pass_on(which_y, which_z, way):
        piece = block(which_y, which_z)
        return send(piece, piece, up if way == 0 else down)

    ring = {}
    mine = [y, 1 - y]
    across = send(block(y, z), block(y, z), other_y)
    for way in range(2):
        ring[way, 0, 0] = pass_on(y, z, way)
    arrive(across, block(1 - y, z), other_y)
    for way in range(2):
        ring[way, 0, 1] = pass_on(1 - y, z, way)
    to_core(y, z)
    to_core(1 - y, z)
    for step in range(1, 5):
        for k in range(2):
            for way in range(2):
                if step == 4 and way != k:
                    continue
                came = lax.rem(z + (8 - step if way == 0 else step), FAR)
                arrive(ring[way, step - 1, k], block(mine[k], came), down if way == 0 else up)
                if step < 3 or (step == 3 and way == k):
                    ring[way, step, k] = pass_on(mine[k], came, way)
                to_core(mine[k], came)

    far_copies = []
    for step in range(1, FAR):
        there = lax.rem(z + step, FAR)
        far_copies.append(send(offset.at[:, there], far_offset.at[z], far_peer(there)))
    own = pltpu.make_async_copy(offset.at[:, z], far_offset.at[z], local_sem.at[1])
    own.start()

    load.wait()
    for number, landing in shares:
        arrive(number, landing, other_core)

    def multiply(slot, target):
        at = pl.ds(pl.multiple_of(target * rows, rows), rows)
        for k in range(PARTS):
            cut = pl.ds(k * wide, wide)
            partial[slot, :, cut] = jnp.dot(
                hidden[0, at, :], weights[:half, cut], preferred_element_type=jnp.float32
            ) + jnp.dot(
                hidden[1, at, :], weights[half:, cut], preferred_element_type=jnp.float32
            )
            yield cut

    first, last = pl.ds(0, mid), pl.ds(mid, mid)
    relays = []
    for k, cut in enumerate(multiply(0, lax.rem(seq + 2, 4))):
        relays.append(
            (
                send(partial.at[0, first, cut], relay_in.at[0, :, cut], after),
                send(partial.at[0, last, cut], relay_in.at[1, :, cut], before),
            )
        )
    directs = []
    for cut in multiply(1, lax.rem(seq + 1, 4)):
        directs.append([send(partial.at[1, last, cut], direct_in.at[0, :, cut], after)])
    for k, cut in enumerate(multiply(2, lax.rem(seq + 3, 4))):
        directs[k].append(send(partial.at[2, first, cut], direct_in.at[1, :, cut], before))
    finals = []
    for k in range(PARTS):
        cut = pl.ds(k * wide, wide)
        arrive(relays[k][0], relay_in.at[0, :, cut], before)
        partial[1, first, cut] += relay_in[0, :, cut]
        one = send(partial.at[1, first, cut], final_in.at[0, :, cut], after)
        arrive(relays[k][1], relay_in.at[1, :, cut], after)
        partial[2, last, cut] += relay_in[1, :, cut]
        finals.append((one, send(partial.at[2, last, cut], final_in.at[1, :, cut], before)))
    for cut in multiply(3, seq):
        pass

    own.wait()
    for step in range(1, FAR):
        source = lax.rem(z + FAR - step, FAR)
        arrive(far_copies[step - 1], far_offset.at[source], far_peer(source))

    def landed(index):
        return near_offset.at[index // 8, :, lax.rem(index, 8)]

    near_copies = []
    for step in range(1, NEAR):
        there = lax.rem(here + step, NEAR)
        near_copies.append(
            send(
                far_offset.at[:, there // 8, lax.rem(there, 8)], landed(here), near_peer(there)
            )
        )
    own = pltpu.make_async_copy(far_offset.at[:, y, pair], landed(here), local_sem.at[2])
    own.start()
    own.wait()
    for step in range(1, NEAR):
        source = lax.rem(here + NEAR - step, NEAR)
        arrive(near_copies[step - 1], landed(source), near_peer(source))

    inverse = 1.0 / divisor[...]
    cooler = 1.0 / softening[...]
    highest = None
    for k in range(PARTS):
        cut = pl.ds(k * wide, wide)
        arrive(directs[k][0], direct_in.at[0, :, cut], before)
        arrive(directs[k][1], direct_in.at[1, :, cut], after)
        arrive(finals[k][0], final_in.at[0, :, cut], before)
        arrive(finals[k][1], final_in.at[1, :, cut], after)
        for j in range(k * wide // 128, (k + 1) * wide // 128):
            at = pl.ds(j * 128, 128)
            upper = partial[3, first, at] + (final_in[0, :, at] + direct_in[1, :, at])
            lower = partial[3, last, at] + (final_in[1, :, at] + direct_in[0, :, at])
            raw = jnp.concatenate([upper, lower])
            shift = near_offset[:, :, :, j, :].reshape(rows, 128)
            scaled = jnp.where(raw > 0, raw * inverse, raw * divisor[...])
            changed = jnp.where(shift < 0, scaled, raw) + shift
            out[:, at] = changed.astype(jnp.bfloat16)
            turned = (changed * cooler).T
            scores[at, :] = turned
            most = jnp.max(turned, axis=0, keepdims=True)
            highest = most if highest is None else jnp.maximum(highest, most)

    def sems(turn):
        return (
            sem_near_send.at[turn],
            sem_near_recv.at[turn],
            sem_far_send.at[turn],
            sem_far_recv.at[turn],
        )

    largest, more = reduced(highest, near_a, far_a, sems(0), jnp.maximum)
    sent += more
    total = jnp.zeros((8, 128), jnp.float32)
    chunk = 64
    for k in range(scores.shape[0] // chunk):
        at = pl.ds(k * chunk, chunk)
        grown = jnp.exp(scores[at, :] - largest)
        terms[at, :] = grown
        total = total + jnp.sum(grown.reshape(chunk // 8, 8, 128), axis=0)

    first = [largest - (SPAN / (LEVELS[0] + 1)) * (k + 1) for k in range(LEVELS[0])]
    rows = [jnp.sum(total, axis=0, keepdims=True)] + masses(scores, terms, first)
    sums, more = reduced(jnp.concatenate(rows), near_b, far_b, sems(1), jnp.add)
    sent += more
    target = share[...] * sums[0:1]
    lower = jnp.sum(
        jnp.where(sums[1:] < target, 1.0, 0.0), axis=0, keepdims=True
    ) * (LEVELS[1] + 1)

    unit = SPAN / ((LEVELS[0] + 1) * (LEVELS[1] + 1))
    second = [largest - unit * (lower + (k + 1)) for k in range(LEVELS[1])]
    rows = masses(scores, terms, second)
    rows.append(rows[-1])
    sums, more = reduced(jnp.concatenate(rows), near_c, far_c, sems(2), jnp.add)
    sent += more
    below = jnp.where(sums[: LEVELS[1]] < target, 1.0, 0.0)
    lower = lower + jnp.sum(below, axis=0, keepdims=True)
    cutoff[...] = largest - unit * (lower + 1.0)
    for copy in sent:
        copy.wait_send()


def step(latent, weights, offset, divisor, softening, share, rows):
    columns = weights.shape[1]
    vmem = pl.BlockSpec(memory_space=pltpu.VMEM)
    depth = weights.shape[0]

    def held(count, lines):
        return pltpu.VMEM((count, lines, 128), jnp.float32)

    def whole(*shape):
        return pltpu.VMEM(shape, jnp.float32)

    return pl.pallas_call(
        step_kernel,
        out_shape=(
            jax.ShapeDtypeStruct((rows, columns), jnp.bfloat16),
            jax.ShapeDtypeStruct((1, rows), jnp.float32),
        ),
        in_specs=[vmem, pl.BlockSpec(memory_space=pl.ANY)] + [vmem] * 4,
        out_specs=(vmem, vmem),
        scratch_shapes=[
            pltpu.VMEM((depth, columns), weights.dtype),
            pltpu.VMEM((8, latent.shape[0], depth // 2), latent.dtype),
            pltpu.VMEM((2, 4 * rows, depth // 2), latent.dtype),
            whole(4, rows, columns),
            whole(2, rows // 2, columns),
            whole(2, rows // 2, columns),
            whole(2, rows // 2, columns),
            whole(FAR, 2, 8, columns // 128, 128),
            whole(2, FAR, 8, columns // 128, 128),
            whole(columns, rows),
            whole(columns, rows),
            held(NEAR, 1),
            held(FAR, 1),
            held(NEAR, LEVELS[0] + 1),
            held(FAR, LEVELS[0] + 1),
            held(NEAR, LEVELS[1] + 1),
            held(FAR, LEVELS[1] + 1),
            pltpu.SemaphoreType.DMA((COPIES,)),
            pltpu.SemaphoreType.DMA((COPIES,)),
            pltpu.SemaphoreType.DMA((3,)),
            pltpu.SemaphoreType.DMA((3, NEAR)),
            pltpu.SemaphoreType.DMA((3, NEAR)),
            pltpu.SemaphoreType.DMA((3, FAR)),
            pltpu.SemaphoreType.DMA((3, FAR)),
        ],
        compiler_params=pltpu.CompilerParams(
            collective_id=1, has_side_effects=True, vmem_limit_bytes=56 * 2**20
        ),
        name="step",
    )(latent, weights, offset, divisor[:, None], softening[:, None], share[None, :])


def per_device(
    latent_vector,
    unembedding_matrix,
    occurrence_tally,
    additive_offset_table,
    recurrence_charge,
    appearance_charge,
    recurrence_divisor,
    softening_divisor,
    nucleus_share_limit,
):
    count_float = occurrence_tally.astype(jnp.float32)
    offset = (
        additive_offset_table.astype(jnp.float32)
        - recurrence_charge[:, None] * count_float
        - appearance_charge[:, None] * (occurrence_tally > 0).astype(jnp.float32)
    )
    rows = recurrence_divisor.shape[0]
    offset = lax.reduce_precision(offset, 8, 7).reshape(2, FAR, 8, -1, 128)
    out, cutoff = step(
        latent_vector,
        unembedding_matrix,
        offset,
        recurrence_divisor,
        softening_divisor,
        nucleus_share_limit,
        rows,
    )
    return out, cutoff.reshape(-1)


def solution(mesh):
    split = Mesh(
        mesh.devices.reshape(2, 8, 4, 2, mesh.shape["seq"]),
        ("vocab_0", "vocab_1", "vocab_2", "vocab_3", "seq"),
    )
    placed = (
        P(VOCAB, "seq"),
        P("seq", VOCAB),
        P(SEQ_VOCAB, None),
        P(SEQ_VOCAB, None),
        P(SEQ_VOCAB),
        P(SEQ_VOCAB),
        P("seq"),
        P("seq"),
        P("seq"),
    )
    return jax.shard_map(
        per_device,
        mesh=split,
        in_specs=placed,
        out_specs=(P("seq", VOCAB), P("seq")),
        check_vma=False,
    )
```

```python
import itertools

import jax
import jax.numpy as jnp
from jax import lax
from jax.experimental import pallas as pl
from jax.experimental.pallas import tpu as pltpu
from jax.sharding import Mesh
from jax.sharding import PartitionSpec as P

VOCAB = ("vocab_0", "vocab_1", "vocab_2", "vocab_3")
SEQ_VOCAB = ("seq", "vocab_0", "vocab_1", "vocab_2", "vocab_3")
MESH = pl.DeviceIdType.MESH
NEAR = 16
FAR = 8
LEVELS = (31, 15)
SPAN = 32.0
PARTS = 4
GROUP = 32
COPIES = 112


def near_index():
    return (
        lax.axis_index("vocab_0") * 8
        + lax.axis_index("vocab_2") * 2
        + lax.axis_index("vocab_3")
    )


def near_peer(index):
    return {
        "vocab_0": index // 8,
        "vocab_2": lax.rem(index // 2, 4),
        "vocab_3": lax.rem(index, 2),
    }


def group_peer(index):
    return {
        "vocab_0": index // 16,
        "vocab_1": lax.rem(index // 2, 8),
        "vocab_3": lax.rem(index, 2),
    }


def far_peer(index):
    return {"vocab_1": index}


def exchange(held, me, count, peer, send_sem, recv_sem):
    copies = []
    for step in range(1, count):
        there = lax.rem(me + step, count)
        copy = pltpu.make_async_remote_copy(
            src_ref=held.at[me],
            dst_ref=held.at[me],
            send_sem=send_sem.at[step],
            recv_sem=recv_sem.at[step],
            device_id=peer(there),
            device_id_type=MESH,
        )
        copy.start()
        copies.append(copy)
    for step in range(1, count):
        source = lax.rem(me + count - step, count)
        pltpu.make_async_remote_copy(
            src_ref=held.at[me],
            dst_ref=held.at[source],
            send_sem=send_sem.at[step],
            recv_sem=recv_sem.at[step],
            device_id=peer(source),
            device_id_type=MESH,
        ).wait_recv()
    return copies


def reduced(values, near, far, sems, combine):
    here, there = near_index(), lax.axis_index("vocab_1")
    near[here] = values
    sent = exchange(near, here, NEAR, near_peer, sems[0], sems[1])
    part = near[0]
    for k in range(1, NEAR):
        part = combine(part, near[k])
    far[there] = part
    sent += exchange(far, there, FAR, far_peer, sems[2], sems[3])
    whole = far[0]
    for k in range(1, FAR):
        whole = combine(whole, far[k])
    return whole, sent


def masses(scores, weights, limits):
    rows = []
    chunks = scores.shape[0] // 8
    for start in range(0, len(limits), 8):
        group = [jnp.broadcast_to(t, (8, 128)) for t in limits[start : start + 8]]

        def add(k, sums, group=group):
            at = pl.ds(pl.multiple_of(k * 8, 8), 8)
            s, w = scores[at, :], weights[at, :]
            return tuple(a + jnp.where(s >= t, w, 0.0) for a, t in zip(sums, group))

        zero = jnp.zeros((8, 128), jnp.float32)
        sums = lax.fori_loop(0, chunks, add, (zero,) * len(group), unroll=8)
        rows += [jnp.sum(a, axis=0, keepdims=True) for a in sums]
    return rows


def step_kernel(
    latent,
    weights_hbm,
    tally,
    table,
    charge,
    appearance,
    divisor,
    softening,
    share,
    out,
    cutoff,
    weights,
    offset,
    few,
    hidden,
    partial,
    relay_in,
    direct_in,
    final_in,
    far_offset,
    near_offset,
    scores,
    terms,
    near_a,
    far_a,
    near_b,
    far_b,
    near_c,
    far_c,
    send_sem,
    recv_sem,
    local_sem,
    sem_near_send,
    sem_near_recv,
    sem_far_send,
    sem_far_recv,
):
    y, z = lax.axis_index("vocab_0"), lax.axis_index("vocab_1")
    x, core = lax.axis_index("vocab_2"), lax.axis_index("vocab_3")
    seq = lax.axis_index("seq")
    here, pair = near_index(), x * 2 + core
    half = latent.shape[1] // 2
    rows, columns = out.shape
    mid, wide = rows // 2, columns // PARTS

    load = pltpu.make_async_copy(weights_hbm, weights, local_sem.at[0])
    load.start()
    barrier = pltpu.get_barrier_semaphore()

    def greet(peer):
        pl.semaphore_signal(barrier, inc=1, device_id=peer, device_id_type=MESH)

    group = (y * FAR + z) * 2 + core
    for step in range(1, GROUP):
        greet(group_peer(lax.rem(group + step, GROUP)))
    for step in range(1, NEAR):
        greet(near_peer(lax.rem(here + step, NEAR)))
    after, before = {"seq": lax.rem(seq + 1, 4)}, {"seq": lax.rem(seq + 3, 4)}
    greet(after)
    greet(before)

    numbers = itertools.count()
    sent = []

    def describe(number, source, target, peer):
        return pltpu.make_async_remote_copy(
            src_ref=source,
            dst_ref=target,
            send_sem=send_sem.at[number],
            recv_sem=recv_sem.at[number],
            device_id=peer,
            device_id_type=MESH,
        )

    def send(source, target, peer):
        number = next(numbers)
        copy = describe(number, source, target, peer)
        copy.start()
        sent.append(copy)
        return number

    def arrive(number, landing, peer):
        describe(number, landing, landing, peer).wait_recv()

    def my_half(which):
        return pl.ds(pl.multiple_of(which * half, 128), half)

    few[group] = latent[:, my_half(core)]
    pl.semaphore_wait(barrier, NEAR + GROUP)

    swaps = []
    for step in range(1, GROUP):
        there = lax.rem(group + step, GROUP)
        swaps.append(
            send(latent.at[:, my_half(lax.rem(there, 2))], few.at[group], group_peer(there))
        )

    flat = offset.reshape(tally.shape[0], 128)
    lines = 64
    each = jnp.broadcast_to(charge[...], (lines, 128))
    once = jnp.broadcast_to(appearance[...], (lines, 128))

    def shift_lines(k, carry):
        base = pl.multiple_of(k * lines, lines)
        line = table[:, pl.ds(pl.multiple_of(base * 128, lines * 128), lines * 128)]
        line = line.astype(jnp.float32)
        for j in range(lines):
            flat[pl.ds(base + j, 1), :] = line[:, j * 128 : (j + 1) * 128]
        at = pl.ds(base, lines)
        count = tally[at, :].astype(jnp.float32)
        value = (
            flat[at, :] - each * count - once * jnp.where(count > 0, 1.0, 0.0)
        )
        flat[at, :] = value.astype(jnp.bfloat16).astype(jnp.float32)
        return carry

    lax.fori_loop(0, tally.shape[0] // lines, shift_lines, 0)

    for step in range(1, GROUP):
        source = lax.rem(group + GROUP - step, GROUP)
        arrive(swaps[step - 1], few.at[source], group_peer(source))

    other_core = {"vocab_3": 1 - core}
    strip = rows // 4
    targets = [lax.rem(seq + k, 4) for k in (2, 1, 3, 0)]

    def block(side, which_x, target):
        at = pl.multiple_of(target * strip, strip)
        return hidden.at[side, which_x, pl.ds(at, strip)]

    for k in range(4):
        joined = [few[k * 8 + j].astype(jnp.float32) for j in range(8)]
        hidden[core, x, pl.ds(k * strip, strip)] = jnp.concatenate(joined).astype(jnp.bfloat16)

    shares, lines_sent = [[] for _ in targets], []

    def to_core(k, which_x):
        piece = block(core, which_x, targets[k])
        shares[k].append((send(piece, piece, other_core), which_x))

    for k, target in enumerate(targets):
        piece = block(core, x, target)
        lines_sent.append(
            [
                send(piece, piece, {"vocab_2": lax.rem(x + step, 4)})
                for step in (2, 1, 3)
            ]
        )
        to_core(k, x)

    def ready(k):
        for number, step in zip(lines_sent[k], (2, 1, 3)):
            source = lax.rem(x + 4 - step, 4)
            arrive(number, block(core, source, targets[k]), {"vocab_2": source})
            to_core(k, source)
        for number, which_x in shares[k]:
            arrive(number, block(1 - core, which_x, targets[k]), other_core)

    def multiply(slot, target):
        at = pl.ds(pl.multiple_of(target * strip, strip), strip)
        for k in range(PARTS):
            cut = pl.ds(k * wide, wide)
            total = jnp.dot(
                hidden[0, :, at, :].reshape(rows, half),
                weights[:half, cut],
                preferred_element_type=jnp.float32,
            ) + jnp.dot(
                hidden[1, :, at, :].reshape(rows, half),
                weights[half:, cut],
                preferred_element_type=jnp.float32,
            )
            for i in range(4):
                for j in range(4):
                    partial[slot, pl.ds((j * 4 + i) * 8, 8), cut] = total[
                        (i * 4 + j) * 8 : (i * 4 + j + 1) * 8
                    ]
            yield cut

    first, last = pl.ds(0, mid), pl.ds(mid, mid)
    relays = []
    ready(0)
    load.wait()
    for k, cut in enumerate(multiply(0, targets[0])):
        relays.append(
            (
                send(partial.at[0, first, cut], relay_in.at[0, :, cut], after),
                send(partial.at[0, last, cut], relay_in.at[1, :, cut], before),
            )
        )
    directs = []
    ready(1)
    for cut in multiply(1, targets[1]):
        directs.append([send(partial.at[1, last, cut], direct_in.at[0, :, cut], after)])
    ready(2)
    for k, cut in enumerate(multiply(2, targets[2])):
        directs[k].append(send(partial.at[2, first, cut], direct_in.at[1, :, cut], before))

    far_copies = []
    for step in range(1, FAR):
        there = lax.rem(z + step, FAR)
        far_copies.append(send(offset.at[:, there], far_offset.at[z], far_peer(there)))
    own = pltpu.make_async_copy(offset.at[:, z], far_offset.at[z], local_sem.at[1])
    own.start()

    finals = []
    for k in range(PARTS):
        cut = pl.ds(k * wide, wide)
        arrive(relays[k][0], relay_in.at[0, :, cut], before)
        partial[1, first, cut] += relay_in[0, :, cut]
        one = send(partial.at[1, first, cut], final_in.at[0, :, cut], after)
        arrive(relays[k][1], relay_in.at[1, :, cut], after)
        partial[2, last, cut] += relay_in[1, :, cut]
        finals.append((one, send(partial.at[2, last, cut], final_in.at[1, :, cut], before)))
    ready(3)
    for cut in multiply(3, targets[3]):
        pass

    own.wait()
    for step in range(1, FAR):
        source = lax.rem(z + FAR - step, FAR)
        arrive(far_copies[step - 1], far_offset.at[source], far_peer(source))

    def landed(index):
        return near_offset.at[index // 8, :, lax.rem(index, 8)]

    near_copies = []
    for step in range(1, NEAR):
        there = lax.rem(here + step, NEAR)
        near_copies.append(
            send(
                far_offset.at[:, there // 8, lax.rem(there, 8)], landed(here), near_peer(there)
            )
        )
    own = pltpu.make_async_copy(far_offset.at[:, y, pair], landed(here), local_sem.at[2])
    own.start()
    own.wait()
    for step in range(1, NEAR):
        source = lax.rem(here + NEAR - step, NEAR)
        arrive(near_copies[step - 1], landed(source), near_peer(source))

    factor = jnp.broadcast_to(divisor[...], (128, rows)).T
    inverse = 1.0 / factor
    cooler = 1.0 / jnp.broadcast_to(softening[...], (128, rows)).T
    highest = None
    for k in range(PARTS):
        cut = pl.ds(k * wide, wide)
        arrive(directs[k][0], direct_in.at[0, :, cut], before)
        arrive(directs[k][1], direct_in.at[1, :, cut], after)
        arrive(finals[k][0], final_in.at[0, :, cut], before)
        arrive(finals[k][1], final_in.at[1, :, cut], after)
        for j in range(k * wide // 128, (k + 1) * wide // 128):
            at = pl.ds(j * 128, 128)
            upper = partial[3, first, at] + (final_in[0, :, at] + direct_in[1, :, at])
            lower = partial[3, last, at] + (final_in[1, :, at] + direct_in[0, :, at])
            raw = jnp.concatenate([upper, lower])
            shift = near_offset[:, :, :, j, :].reshape(rows, 128)
            scaled = jnp.where(raw > 0, raw * inverse, raw * factor)
            changed = jnp.where(shift < 0, scaled, raw) + shift
            out[:, at] = changed.astype(jnp.bfloat16)
            turned = (changed * cooler).T
            scores[at, :] = turned
            most = jnp.max(turned, axis=0, keepdims=True)
            highest = most if highest is None else jnp.maximum(highest, most)

    def sems(turn):
        return (
            sem_near_send.at[turn],
            sem_near_recv.at[turn],
            sem_far_send.at[turn],
            sem_far_recv.at[turn],
        )

    largest, more = reduced(highest, near_a, far_a, sems(0), jnp.maximum)
    sent += more
    total = jnp.zeros((8, 128), jnp.float32)
    chunk = 64
    for k in range(scores.shape[0] // chunk):
        at = pl.ds(k * chunk, chunk)
        grown = jnp.exp(scores[at, :] - largest)
        terms[at, :] = grown
        total = total + jnp.sum(grown.reshape(chunk // 8, 8, 128), axis=0)

    first = [largest - (SPAN / (LEVELS[0] + 1)) * (k + 1) for k in range(LEVELS[0])]
    rows = [jnp.sum(total, axis=0, keepdims=True)] + masses(scores, terms, first)
    sums, more = reduced(jnp.concatenate(rows), near_b, far_b, sems(1), jnp.add)
    sent += more
    target = share[...] * sums[0:1]
    lower = jnp.sum(
        jnp.where(sums[1:] < target, 1.0, 0.0), axis=0, keepdims=True
    ) * (LEVELS[1] + 1)

    unit = SPAN / ((LEVELS[0] + 1) * (LEVELS[1] + 1))
    second = [largest - unit * (lower + (k + 1)) for k in range(LEVELS[1])]
    rows = masses(scores, terms, second)
    rows.append(rows[-1])
    sums, more = reduced(jnp.concatenate(rows), near_c, far_c, sems(2), jnp.add)
    sent += more
    below = jnp.where(sums[: LEVELS[1]] < target, 1.0, 0.0)
    lower = lower + jnp.sum(below, axis=0, keepdims=True)
    cutoff[...] = largest - unit * (lower + 1.0)
    for copy in sent:
        copy.wait_send()


def settle_kernel(out, cutoff, out_kept, cutoff_kept):
    out_kept[...] = out[...]
    cutoff_kept[...] = cutoff[...]


def step(latent, weights, tally, table, charge, appearance, *by_row):
    depth, columns = weights.shape
    rows = by_row[0].shape[0]
    vmem = pl.BlockSpec(memory_space=pltpu.VMEM)

    def held(count, lines):
        return pltpu.VMEM((count, lines, 128), jnp.float32)

    def whole(*shape):
        return pltpu.VMEM(shape, jnp.float32)

    results = (
        jax.ShapeDtypeStruct((rows, columns), jnp.bfloat16),
        jax.ShapeDtypeStruct((1, rows), jnp.float32),
    )
    found = pl.pallas_call(
        step_kernel,
        out_shape=results,
        in_specs=[vmem, pl.BlockSpec(memory_space=pl.ANY)] + [vmem] * 7,
        out_specs=(vmem, vmem),
        scratch_shapes=[
            pltpu.VMEM((depth, columns), weights.dtype),
            whole(2, FAR, 8, columns // 128, 128),
            pltpu.VMEM((GROUP, latent.shape[0], depth // 2), latent.dtype),
            pltpu.VMEM((2, 4, rows, depth // 2), latent.dtype),
            whole(4, rows, columns),
            whole(2, rows // 2, columns),
            whole(2, rows // 2, columns),
            whole(2, rows // 2, columns),
            whole(FAR, 2, 8, columns // 128, 128),
            whole(2, FAR, 8, columns // 128, 128),
            whole(columns, rows),
            whole(columns, rows),
            held(NEAR, 1),
            held(FAR, 1),
            held(NEAR, LEVELS[0] + 1),
            held(FAR, LEVELS[0] + 1),
            held(NEAR, LEVELS[1] + 1),
            held(FAR, LEVELS[1] + 1),
            pltpu.SemaphoreType.DMA((COPIES,)),
            pltpu.SemaphoreType.DMA((COPIES,)),
            pltpu.SemaphoreType.DMA((3,)),
            pltpu.SemaphoreType.DMA((3, NEAR)),
            pltpu.SemaphoreType.DMA((3, NEAR)),
            pltpu.SemaphoreType.DMA((3, FAR)),
            pltpu.SemaphoreType.DMA((3, FAR)),
        ],
        compiler_params=pltpu.CompilerParams(
            collective_id=1, has_side_effects=True, vmem_limit_bytes=56 * 2**20
        ),
        name="step",
    )(
        latent,
        weights,
        tally.reshape(-1, 128),
        table,
        charge[None, :],
        appearance[None, :],
        *(part[None, :] for part in by_row),
    )
    return pl.pallas_call(
        settle_kernel,
        out_shape=results,
        in_specs=[vmem, vmem],
        out_specs=(vmem, vmem),
        name="settle",
    )(*found)


def per_device(*arguments):
    out, cutoff = step(*arguments)
    return out, cutoff.reshape(-1)


def solution(mesh):
    split = Mesh(
        mesh.devices.reshape(2, 8, 4, 2, mesh.shape["seq"]),
        ("vocab_0", "vocab_1", "vocab_2", "vocab_3", "seq"),
    )
    placed = (
        P(VOCAB, "seq"),
        P("seq", VOCAB),
        P(SEQ_VOCAB, None),
        P(SEQ_VOCAB, None),
        P(SEQ_VOCAB),
        P(SEQ_VOCAB),
        P("seq"),
        P("seq"),
        P("seq"),
    )
    return jax.shard_map(
        per_device,
        mesh=split,
        in_specs=placed,
        out_specs=(P("seq", VOCAB), P("seq")),
        check_vma=False,
    )
```

```python
import itertools

import jax
import jax.numpy as jnp
from jax import lax
from jax.experimental import pallas as pl
from jax.experimental.pallas import tpu as pltpu
from jax.sharding import Mesh
from jax.sharding import PartitionSpec as P

VOCAB = ("vocab_0", "vocab_1", "vocab_2", "vocab_3")
SEQ_VOCAB = ("seq", "vocab_0", "vocab_1", "vocab_2", "vocab_3")
MESH = pl.DeviceIdType.MESH
NEAR = 16
FAR = 8
LEVELS = (31, 15)
SPAN = 32.0
PARTS = 4
GROUP = 32
COPIES = 112
LIMIT = 524280.0


def near_index():
    return (
        lax.axis_index("vocab_0") * 8
        + lax.axis_index("vocab_2") * 2
        + lax.axis_index("vocab_3")
    )


def near_peer(index):
    return {
        "vocab_0": index // 8,
        "vocab_2": lax.rem(index // 2, 4),
        "vocab_3": lax.rem(index, 2),
    }


def group_peer(index):
    return {
        "vocab_0": index // 16,
        "vocab_1": lax.rem(index // 2, 8),
        "vocab_3": lax.rem(index, 2),
    }


def far_peer(index):
    return {"vocab_1": index}


def exchange(held, me, count, peer, send_sem, recv_sem):
    copies = []
    for step in range(1, count):
        there = lax.rem(me + step, count)
        copy = pltpu.make_async_remote_copy(
            src_ref=held.at[me],
            dst_ref=held.at[me],
            send_sem=send_sem.at[step],
            recv_sem=recv_sem.at[step],
            device_id=peer(there),
            device_id_type=MESH,
        )
        copy.start()
        copies.append(copy)
    for step in range(1, count):
        source = lax.rem(me + count - step, count)
        pltpu.make_async_remote_copy(
            src_ref=held.at[me],
            dst_ref=held.at[source],
            send_sem=send_sem.at[step],
            recv_sem=recv_sem.at[step],
            device_id=peer(source),
            device_id_type=MESH,
        ).wait_recv()
    return copies


def reduced(values, near, far, sems, combine):
    here, there = near_index(), lax.axis_index("vocab_1")
    near[here] = values
    sent = exchange(near, here, NEAR, near_peer, sems[0], sems[1])
    part = near[0]
    for k in range(1, NEAR):
        part = combine(part, near[k])
    far[there] = part
    sent += exchange(far, there, FAR, far_peer, sems[2], sems[3])
    whole = far[0]
    for k in range(1, FAR):
        whole = combine(whole, far[k])
    return whole, sent


def masses(scores, weights, limits):
    rows = []
    chunks = scores.shape[0] // 8
    for start in range(0, len(limits), 8):
        group = [jnp.broadcast_to(t, (8, 128)) for t in limits[start : start + 8]]

        def add(k, sums, group=group):
            at = pl.ds(pl.multiple_of(k * 8, 8), 8)
            s, w = scores[at, :], weights[at, :]
            return tuple(a + jnp.where(s >= t, w, 0.0) for a, t in zip(sums, group))

        zero = jnp.zeros((8, 128), jnp.float32)
        sums = lax.fori_loop(0, chunks, add, (zero,) * len(group), unroll=8)
        rows += [jnp.sum(a, axis=0, keepdims=True) for a in sums]
    return rows


def step_kernel(
    latent,
    weights_hbm,
    tally,
    table,
    charge,
    appearance,
    divisor,
    softening,
    share,
    out,
    cutoff,
    weights,
    offset,
    few,
    hidden,
    partial,
    coded,
    relay_in,
    direct_in,
    final_in,
    scale_out,
    scale_in,
    far_offset,
    near_offset,
    scores,
    terms,
    near_a,
    far_a,
    near_b,
    far_b,
    near_c,
    far_c,
    send_sem,
    recv_sem,
    local_sem,
    sem_near_send,
    sem_near_recv,
    sem_far_send,
    sem_far_recv,
):
    y, z = lax.axis_index("vocab_0"), lax.axis_index("vocab_1")
    x, core = lax.axis_index("vocab_2"), lax.axis_index("vocab_3")
    seq = lax.axis_index("seq")
    here, pair = near_index(), x * 2 + core
    half = latent.shape[1] // 2
    rows, columns = out.shape
    mid, wide = rows // 2, columns // PARTS

    load = pltpu.make_async_copy(weights_hbm, weights, local_sem.at[0])
    load.start()
    barrier = pltpu.get_barrier_semaphore()

    def greet(peer):
        pl.semaphore_signal(barrier, inc=1, device_id=peer, device_id_type=MESH)

    group = (y * FAR + z) * 2 + core
    for step in range(1, GROUP):
        greet(group_peer(lax.rem(group + step, GROUP)))
    for step in range(1, NEAR):
        greet(near_peer(lax.rem(here + step, NEAR)))
    after, before = {"seq": lax.rem(seq + 1, 4)}, {"seq": lax.rem(seq + 3, 4)}
    greet(after)
    greet(before)

    numbers = itertools.count()
    sent = []

    def describe(number, source, target, peer):
        return pltpu.make_async_remote_copy(
            src_ref=source,
            dst_ref=target,
            send_sem=send_sem.at[number],
            recv_sem=recv_sem.at[number],
            device_id=peer,
            device_id_type=MESH,
        )

    def send(source, target, peer):
        number = next(numbers)
        copy = describe(number, source, target, peer)
        copy.start()
        sent.append(copy)
        return number

    def arrive(number, landing, peer):
        describe(number, landing, landing, peer).wait_recv()

    def my_half(which):
        return pl.ds(pl.multiple_of(which * half, 128), half)

    few[group] = latent[:, my_half(core)]
    pl.semaphore_wait(barrier, NEAR + GROUP)

    swaps = []
    for step in range(1, GROUP):
        there = lax.rem(group + step, GROUP)
        swaps.append(
            send(latent.at[:, my_half(lax.rem(there, 2))], few.at[group], group_peer(there))
        )

    flat = offset.reshape(tally.shape[0], 128)
    lines = 64
    each = jnp.broadcast_to(charge[...], (lines, 128))
    once = jnp.broadcast_to(appearance[...], (lines, 128))

    def shift_lines(k, carry):
        base = pl.multiple_of(k * lines, lines)
        line = table[:, pl.ds(pl.multiple_of(base * 128, lines * 128), lines * 128)]
        line = line.astype(jnp.float32)
        for j in range(lines):
            flat[pl.ds(base + j, 1), :] = line[:, j * 128 : (j + 1) * 128]
        at = pl.ds(base, lines)
        count = tally[at, :].astype(jnp.float32)
        value = (
            flat[at, :] - each * count - once * jnp.where(count > 0, 1.0, 0.0)
        )
        flat[at, :] = value.astype(jnp.bfloat16).astype(jnp.float32)
        return carry

    lax.fori_loop(0, tally.shape[0] // lines, shift_lines, 0)

    for step in range(1, GROUP):
        source = lax.rem(group + GROUP - step, GROUP)
        arrive(swaps[step - 1], few.at[source], group_peer(source))

    other_core = {"vocab_3": 1 - core}
    strip = rows // 4
    targets = [lax.rem(seq + k, 4) for k in (2, 1, 3, 0)]

    def block(side, which_x, target):
        at = pl.multiple_of(target * strip, strip)
        return hidden.at[side, which_x, pl.ds(at, strip)]

    for k in range(4):
        joined = [few[k * 8 + j].astype(jnp.float32) for j in range(8)]
        hidden[core, x, pl.ds(k * strip, strip)] = jnp.concatenate(joined).astype(jnp.bfloat16)

    shares, lines_sent = [[] for _ in targets], []

    def to_core(k, which_x):
        piece = block(core, which_x, targets[k])
        shares[k].append((send(piece, piece, other_core), which_x))

    for k, target in enumerate(targets):
        piece = block(core, x, target)
        lines_sent.append(
            [
                send(piece, piece, {"vocab_2": lax.rem(x + step, 4)})
                for step in (2, 1, 3)
            ]
        )
        to_core(k, x)

    def ready(k):
        for number, step in zip(lines_sent[k], (2, 1, 3)):
            source = lax.rem(x + 4 - step, 4)
            arrive(number, block(core, source, targets[k]), {"vocab_2": source})
            to_core(k, source)
        for number, which_x in shares[k]:
            arrive(number, block(1 - core, which_x, targets[k]), other_core)

    def multiply(slot, target):
        at = pl.ds(pl.multiple_of(target * strip, strip), strip)
        for k in range(PARTS):
            cut = pl.ds(k * wide, wide)
            total = jnp.dot(
                hidden[0, :, at, :].reshape(rows, half),
                weights[:half, cut],
                preferred_element_type=jnp.float32,
            ) + jnp.dot(
                hidden[1, :, at, :].reshape(rows, half),
                weights[half:, cut],
                preferred_element_type=jnp.float32,
            )
            for i in range(4):
                for j in range(4):
                    partial[slot, pl.ds((j * 4 + i) * 8, 8), cut] = total[
                        (i * 4 + j) * 8 : (i * 4 + j + 1) * 8
                    ]

    first, last = pl.ds(0, mid), pl.ds(mid, mid)
    def turn(tile):
        return tile.T[0:1, :]

    def spread(line):
        return jnp.broadcast_to(line, (128, rows)).T

    def peak(slot):
        most = jnp.abs(partial[slot, :, pl.ds(0, 128)])
        for k in range(1, columns // 128):
            most = jnp.maximum(most, jnp.abs(partial[slot, :, pl.ds(k * 128, 128)]))
        most = jnp.maximum(jnp.max(most, axis=1, keepdims=True), 1e-30)
        return jnp.broadcast_to(most, (rows, 128))

    def encode(box, cut, value, gain):
        gain = jnp.concatenate([gain] * (value.shape[1] // 128), axis=1)
        whole = jnp.round(value * gain).astype(jnp.int32)
        coded[box, pl.ds(0, mid), cut] = (whole >> 4).astype(jnp.int16)
        low = whole & 15
        packed = low[:quarter]
        for k in range(1, 4):
            packed = packed | (low[k * quarter : (k + 1) * quarter] << (4 * k))
        coded[box, pl.ds(mid, quarter), cut] = (packed - 32768).astype(jnp.int16)
        return coded.at[box, :, cut]

    def decode(box, cut, unit):
        high = box[pl.ds(0, mid), cut].astype(jnp.int32)
        packed = box[pl.ds(mid, quarter), cut].astype(jnp.int32) + 32768
        low = jnp.concatenate([(packed >> (4 * k)) & 15 for k in range(4)])
        value = ((high << 4) + low).astype(jnp.float32)
        return value * jnp.concatenate([unit] * (value.shape[1] // 128), axis=1)

    quarter = mid // 4
    cuts = [pl.ds(k * wide, wide) for k in range(PARTS)]
    relays = []
    ready(0)
    load.wait()
    multiply(0, targets[0])
    peak_0 = peak(0)
    gain = LIMIT / peak_0
    scale_out[0] = turn(peak_0)
    scale_up = send(scale_out.at[0], scale_in.at[0], after)
    scale_down = send(scale_out.at[0], scale_in.at[1], before)
    for cut in cuts:
        one = encode(0, cut, partial[0, first, cut], gain[:mid])
        one = send(one, relay_in.at[0, :, cut], after)
        two = encode(1, cut, partial[0, last, cut], gain[mid:])
        relays.append((one, send(two, relay_in.at[1, :, cut], before)))
    ready(1)
    multiply(1, targets[1])
    peak_1 = peak(1)
    gain = LIMIT / peak_1
    directs = []
    for cut in cuts:
        one = encode(2, cut, partial[1, last, cut], gain[mid:])
        directs.append([send(one, direct_in.at[0, :, cut], after)])
    ready(2)
    multiply(2, targets[2])
    peak_2 = peak(2)
    gain = LIMIT / peak_2
    for k, cut in enumerate(cuts):
        two = encode(3, cut, partial[2, first, cut], gain[:mid])
        directs[k].append(send(two, direct_in.at[1, :, cut], before))

    arrive(scale_up, scale_in.at[0], before)
    arrive(scale_down, scale_in.at[1], after)
    peak_up, peak_down = spread(scale_in[0])[:mid], spread(scale_in[1])[mid:]
    bound_up, bound_down = peak_up + peak_1[:mid], peak_down + peak_2[mid:]
    scale_out[1] = turn(jnp.concatenate([bound_up, peak_1[mid:]]))
    scale_out[2] = turn(jnp.concatenate([peak_2[:mid], bound_down]))
    scale_up = send(scale_out.at[1], scale_in.at[2], after)
    scale_down = send(scale_out.at[2], scale_in.at[3], before)

    far_copies = []
    for step in range(1, FAR):
        there = lax.rem(z + step, FAR)
        far_copies.append(send(offset.at[:, there], far_offset.at[z], far_peer(there)))
    own = pltpu.make_async_copy(offset.at[:, z], far_offset.at[z], local_sem.at[1])
    own.start()

    finals = []
    gain_up, gain_down = LIMIT / bound_up, LIMIT / bound_down
    unit_up, unit_down = peak_up * (1.0 / LIMIT), peak_down * (1.0 / LIMIT)
    for k, cut in enumerate(cuts):
        arrive(relays[k][0], relay_in.at[0, :, cut], before)
        value = partial[1, first, cut] + decode(relay_in.at[0], cut, unit_up)
        one = send(encode(4, cut, value, gain_up), final_in.at[0, :, cut], after)
        arrive(relays[k][1], relay_in.at[1, :, cut], after)
        value = partial[2, last, cut] + decode(relay_in.at[1], cut, unit_down)
        two = send(encode(5, cut, value, gain_down), final_in.at[1, :, cut], before)
        finals.append((one, two))
    ready(3)
    multiply(3, targets[3])

    own.wait()
    for step in range(1, FAR):
        source = lax.rem(z + FAR - step, FAR)
        arrive(far_copies[step - 1], far_offset.at[source], far_peer(source))

    def landed(index):
        return near_offset.at[index // 8, :, lax.rem(index, 8)]

    near_copies = []
    for step in range(1, NEAR):
        there = lax.rem(here + step, NEAR)
        near_copies.append(
            send(
                far_offset.at[:, there // 8, lax.rem(there, 8)], landed(here), near_peer(there)
            )
        )
    own = pltpu.make_async_copy(far_offset.at[:, y, pair], landed(here), local_sem.at[2])
    own.start()
    own.wait()
    for step in range(1, NEAR):
        source = lax.rem(here + NEAR - step, NEAR)
        arrive(near_copies[step - 1], landed(source), near_peer(source))

    factor = spread(divisor[...])
    inverse = 1.0 / factor
    cooler = 1.0 / spread(softening[...])
    arrive(scale_up, scale_in.at[2], before)
    arrive(scale_down, scale_in.at[3], after)
    unit_up = spread(scale_in[2]) * (1.0 / LIMIT)
    unit_down = spread(scale_in[3]) * (1.0 / LIMIT)
    highest = None
    for k, cut in enumerate(cuts):
        arrive(directs[k][0], direct_in.at[0, :, cut], before)
        arrive(directs[k][1], direct_in.at[1, :, cut], after)
        arrive(finals[k][0], final_in.at[0, :, cut], before)
        arrive(finals[k][1], final_in.at[1, :, cut], after)
        for j in range(k * wide // 128, (k + 1) * wide // 128):
            at = pl.ds(j * 128, 128)
            upper = partial[3, first, at] + (
                decode(final_in.at[0], at, unit_up[:mid])
                + decode(direct_in.at[1], at, unit_down[:mid])
            )
            lower = partial[3, last, at] + (
                decode(final_in.at[1], at, unit_down[mid:])
                + decode(direct_in.at[0], at, unit_up[mid:])
            )
            raw = jnp.concatenate([upper, lower])
            shift = near_offset[:, :, :, j, :].reshape(rows, 128)
            scaled = jnp.where(raw > 0, raw * inverse, raw * factor)
            changed = jnp.where(shift < 0, scaled, raw) + shift
            out[:, at] = changed.astype(jnp.bfloat16)
            turned = (changed * cooler).T
            scores[at, :] = turned
            most = jnp.max(turned, axis=0, keepdims=True)
            highest = most if highest is None else jnp.maximum(highest, most)

    def sems(turn):
        return (
            sem_near_send.at[turn],
            sem_near_recv.at[turn],
            sem_far_send.at[turn],
            sem_far_recv.at[turn],
        )

    largest, more = reduced(highest, near_a, far_a, sems(0), jnp.maximum)
    sent += more
    total = jnp.zeros((8, 128), jnp.float32)
    chunk = 64
    for k in range(scores.shape[0] // chunk):
        at = pl.ds(k * chunk, chunk)
        grown = jnp.exp(scores[at, :] - largest)
        terms[at, :] = grown
        total = total + jnp.sum(grown.reshape(chunk // 8, 8, 128), axis=0)

    first = [largest - (SPAN / (LEVELS[0] + 1)) * (k + 1) for k in range(LEVELS[0])]
    rows = [jnp.sum(total, axis=0, keepdims=True)] + masses(scores, terms, first)
    sums, more = reduced(jnp.concatenate(rows), near_b, far_b, sems(1), jnp.add)
    sent += more
    target = share[...] * sums[0:1]
    lower = jnp.sum(
        jnp.where(sums[1:] < target, 1.0, 0.0), axis=0, keepdims=True
    ) * (LEVELS[1] + 1)

    unit = SPAN / ((LEVELS[0] + 1) * (LEVELS[1] + 1))
    second = [largest - unit * (lower + (k + 1)) for k in range(LEVELS[1])]
    rows = masses(scores, terms, second)
    rows.append(rows[-1])
    sums, more = reduced(jnp.concatenate(rows), near_c, far_c, sems(2), jnp.add)
    sent += more
    below = jnp.where(sums[: LEVELS[1]] < target, 1.0, 0.0)
    lower = lower + jnp.sum(below, axis=0, keepdims=True)
    cutoff[...] = largest - unit * (lower + 1.0)
    for copy in sent:
        copy.wait_send()


def settle_kernel(out, cutoff, out_kept, cutoff_kept):
    out_kept[...] = out[...]
    cutoff_kept[...] = cutoff[...]


def step(latent, weights, tally, table, charge, appearance, *by_row):
    depth, columns = weights.shape
    rows = by_row[0].shape[0]
    vmem = pl.BlockSpec(memory_space=pltpu.VMEM)

    def held(count, lines):
        return pltpu.VMEM((count, lines, 128), jnp.float32)

    def whole(*shape):
        return pltpu.VMEM(shape, jnp.float32)

    def boxes(count):
        return pltpu.VMEM((count, rows * 5 // 8, columns), jnp.int16)

    results = (
        jax.ShapeDtypeStruct((rows, columns), jnp.bfloat16),
        jax.ShapeDtypeStruct((1, rows), jnp.float32),
    )
    found = pl.pallas_call(
        step_kernel,
        out_shape=results,
        in_specs=[vmem, pl.BlockSpec(memory_space=pl.ANY)] + [vmem] * 7,
        out_specs=(vmem, vmem),
        scratch_shapes=[
            pltpu.VMEM((depth, columns), weights.dtype),
            whole(2, FAR, 8, columns // 128, 128),
            pltpu.VMEM((GROUP, latent.shape[0], depth // 2), latent.dtype),
            pltpu.VMEM((2, 4, rows, depth // 2), latent.dtype),
            whole(4, rows, columns),
            boxes(6),
            boxes(2),
            boxes(2),
            boxes(2),
            whole(3, 1, 128),
            whole(4, 1, 128),
            whole(FAR, 2, 8, columns // 128, 128),
            whole(2, FAR, 8, columns // 128, 128),
            whole(columns, rows),
            whole(columns, rows),
            held(NEAR, 1),
            held(FAR, 1),
            held(NEAR, LEVELS[0] + 1),
            held(FAR, LEVELS[0] + 1),
            held(NEAR, LEVELS[1] + 1),
            held(FAR, LEVELS[1] + 1),
            pltpu.SemaphoreType.DMA((COPIES,)),
            pltpu.SemaphoreType.DMA((COPIES,)),
            pltpu.SemaphoreType.DMA((3,)),
            pltpu.SemaphoreType.DMA((3, NEAR)),
            pltpu.SemaphoreType.DMA((3, NEAR)),
            pltpu.SemaphoreType.DMA((3, FAR)),
            pltpu.SemaphoreType.DMA((3, FAR)),
        ],
        compiler_params=pltpu.CompilerParams(
            collective_id=1, has_side_effects=True, vmem_limit_bytes=56 * 2**20
        ),
        name="step",
    )(
        latent,
        weights,
        tally.reshape(-1, 128),
        table,
        charge[None, :],
        appearance[None, :],
        *(part[None, :] for part in by_row),
    )
    return pl.pallas_call(
        settle_kernel,
        out_shape=results,
        in_specs=[vmem, vmem],
        out_specs=(vmem, vmem),
        name="settle",
    )(*found)


def per_device(*arguments):
    out, cutoff = step(*arguments)
    return out, cutoff.reshape(-1)


def solution(mesh):
    split = Mesh(
        mesh.devices.reshape(2, 8, 4, 2, mesh.shape["seq"]),
        ("vocab_0", "vocab_1", "vocab_2", "vocab_3", "seq"),
    )
    placed = (
        P(VOCAB, "seq"),
        P("seq", VOCAB),
        P(SEQ_VOCAB, None),
        P(SEQ_VOCAB, None),
        P(SEQ_VOCAB),
        P(SEQ_VOCAB),
        P("seq"),
        P("seq"),
        P("seq"),
    )
    return jax.shard_map(
        per_device,
        mesh=split,
        in_specs=placed,
        out_specs=(P("seq", VOCAB), P("seq")),
        check_vma=False,
    )
```

```python
import itertools

import jax
import jax.numpy as jnp
from jax import lax
from jax.experimental import pallas as pl
from jax.experimental.pallas import tpu as pltpu
from jax.sharding import Mesh
from jax.sharding import PartitionSpec as P

VOCAB = ("vocab_0", "vocab_1", "vocab_2", "vocab_3")
SEQ_VOCAB = ("seq", "vocab_0", "vocab_1", "vocab_2", "vocab_3")
MESH = pl.DeviceIdType.MESH
NEAR = 16
FAR = 8
LEVELS = (31, 15)
SPAN = 32.0
PARTS = 4
GROUP = 32
COPIES = 112
LIMIT = 524280.0


def near_index():
    return (
        lax.axis_index("vocab_0") * 8
        + lax.axis_index("vocab_2") * 2
        + lax.axis_index("vocab_3")
    )


def near_peer(index):
    return {
        "vocab_0": index // 8,
        "vocab_2": lax.rem(index // 2, 4),
        "vocab_3": lax.rem(index, 2),
    }


def group_peer(index):
    return {
        "vocab_0": index // 16,
        "vocab_1": lax.rem(index // 2, 8),
        "vocab_3": lax.rem(index, 2),
    }


def pair_peer(index):
    return {"vocab_2": index // 2, "vocab_3": lax.rem(index, 2)}


def far_peer(index):
    return {"vocab_1": index}


def exchange(held, me, count, peer, send_sem, recv_sem):
    copies = []
    for step in range(1, count):
        there = lax.rem(me + step, count)
        copy = pltpu.make_async_remote_copy(
            src_ref=held.at[me],
            dst_ref=held.at[me],
            send_sem=send_sem.at[step],
            recv_sem=recv_sem.at[step],
            device_id=peer(there),
            device_id_type=MESH,
        )
        copy.start()
        copies.append(copy)
    for step in range(1, count):
        source = lax.rem(me + count - step, count)
        pltpu.make_async_remote_copy(
            src_ref=held.at[me],
            dst_ref=held.at[source],
            send_sem=send_sem.at[step],
            recv_sem=recv_sem.at[step],
            device_id=peer(source),
            device_id_type=MESH,
        ).wait_recv()
    return copies


def reduced(values, near, far, sems, combine):
    here, there = near_index(), lax.axis_index("vocab_1")
    near[here] = values
    sent = exchange(near, here, NEAR, near_peer, sems[0], sems[1])
    part = near[0]
    for k in range(1, NEAR):
        part = combine(part, near[k])
    far[there] = part
    sent += exchange(far, there, FAR, far_peer, sems[2], sems[3])
    whole = far[0]
    for k in range(1, FAR):
        whole = combine(whole, far[k])
    return whole, sent


def masses(scores, weights, limits):
    rows = []
    chunks = scores.shape[0] // 8
    for start in range(0, len(limits), 8):
        group = [jnp.broadcast_to(t, (8, 128)) for t in limits[start : start + 8]]

        def add(k, sums, group=group):
            at = pl.ds(pl.multiple_of(k * 8, 8), 8)
            s, w = scores[at, :], weights[at, :]
            return tuple(a + jnp.where(s >= t, w, 0.0) for a, t in zip(sums, group))

        zero = jnp.zeros((8, 128), jnp.float32)
        sums = lax.fori_loop(0, chunks, add, (zero,) * len(group), unroll=8)
        rows += [jnp.sum(a, axis=0, keepdims=True) for a in sums]
    return rows


def step_kernel(
    latent,
    weights_hbm,
    tally,
    table,
    charge,
    appearance,
    divisor,
    softening,
    share,
    out,
    cutoff,
    weights,
    offset,
    few,
    hidden,
    partial,
    coded,
    relay_in,
    direct_in,
    final_in,
    scale_out,
    scale_in,
    offset_out,
    offset_pair,
    far_offset,
    near_offset,
    changed_out,
    scores,
    terms,
    near_a,
    far_a,
    near_b,
    far_b,
    near_c,
    far_c,
    send_sem,
    recv_sem,
    local_sem,
    sem_near_send,
    sem_near_recv,
    sem_far_send,
    sem_far_recv,
):
    y, z = lax.axis_index("vocab_0"), lax.axis_index("vocab_1")
    x, core = lax.axis_index("vocab_2"), lax.axis_index("vocab_3")
    seq = lax.axis_index("seq")
    here, pair = near_index(), x * 2 + core
    half = latent.shape[1] // 2
    rows, columns = out.shape
    mid, wide = rows // 2, columns // PARTS

    load = pltpu.make_async_copy(weights_hbm, weights, local_sem.at[0])
    load.start()
    barrier = pltpu.get_barrier_semaphore()

    def greet(peer):
        pl.semaphore_signal(barrier, inc=1, device_id=peer, device_id_type=MESH)

    group = (y * FAR + z) * 2 + core
    for step in range(1, GROUP):
        greet(group_peer(lax.rem(group + step, GROUP)))
    for step in range(1, NEAR):
        greet(near_peer(lax.rem(here + step, NEAR)))
    after, before = {"seq": lax.rem(seq + 1, 4)}, {"seq": lax.rem(seq + 3, 4)}
    greet(after)
    greet(before)

    numbers = itertools.count()
    sent = []

    def describe(number, source, target, peer):
        return pltpu.make_async_remote_copy(
            src_ref=source,
            dst_ref=target,
            send_sem=send_sem.at[number],
            recv_sem=recv_sem.at[number],
            device_id=peer,
            device_id_type=MESH,
        )

    def send(source, target, peer):
        number = next(numbers)
        copy = describe(number, source, target, peer)
        copy.start()
        sent.append(copy)
        return number

    def arrive(number, landing, peer):
        describe(number, landing, landing, peer).wait_recv()

    def my_half(which):
        return pl.ds(pl.multiple_of(which * half, 128), half)

    few[group] = latent[:, my_half(core)]
    pl.semaphore_wait(barrier, NEAR + GROUP)

    swaps = []
    for step in range(1, GROUP):
        there = lax.rem(group + step, GROUP)
        swaps.append(
            send(latent.at[:, my_half(lax.rem(there, 2))], few.at[group], group_peer(there))
        )

    flat = offset.reshape(tally.shape[0], 128)
    lines = 64
    each = jnp.broadcast_to(charge[...], (lines, 128))
    once = jnp.broadcast_to(appearance[...], (lines, 128))

    def shift_lines(k, carry):
        base = pl.multiple_of(k * lines, lines)
        line = table[:, pl.ds(pl.multiple_of(base * 128, lines * 128), lines * 128)]
        line = line.astype(jnp.float32)
        for j in range(lines):
            flat[pl.ds(base + j, 1), :] = line[:, j * 128 : (j + 1) * 128]
        at = pl.ds(base, lines)
        count = tally[at, :].astype(jnp.float32)
        value = (
            flat[at, :] - each * count - once * jnp.where(count > 0, 1.0, 0.0)
        )
        flat[at, :] = value
        return carry

    lax.fori_loop(0, tally.shape[0] // lines, shift_lines, 0)
    other_y = {"vocab_0": 1 - y}
    offset_out[...] = offset[1 - y].astype(jnp.bfloat16)
    offset_pair[y] = offset[y].astype(jnp.bfloat16)
    crossing = send(offset_out, offset_pair.at[y], other_y)

    for step in range(1, GROUP):
        source = lax.rem(group + GROUP - step, GROUP)
        arrive(swaps[step - 1], few.at[source], group_peer(source))

    other_core = {"vocab_3": 1 - core}
    strip = rows // 4
    targets = [lax.rem(seq + k, 4) for k in (2, 1, 3, 0)]

    def block(side, which_x, target):
        at = pl.multiple_of(target * strip, strip)
        return hidden.at[side, which_x, pl.ds(at, strip)]

    for k in range(4):
        joined = [few[k * 8 + j].astype(jnp.float32) for j in range(8)]
        hidden[core, x, pl.ds(k * strip, strip)] = jnp.concatenate(joined).astype(jnp.bfloat16)

    shares, lines_sent = [[] for _ in targets], []

    def to_core(k, which_x):
        piece = block(core, which_x, targets[k])
        shares[k].append((send(piece, piece, other_core), which_x))

    for k, target in enumerate(targets):
        piece = block(core, x, target)
        lines_sent.append(
            [
                send(piece, piece, {"vocab_2": lax.rem(x + step, 4)})
                for step in (2, 1, 3)
            ]
        )
        to_core(k, x)

    arrive(crossing, offset_pair.at[1 - y], other_y)
    far_copies = []
    for step in range(1, FAR):
        there = lax.rem(z + step, FAR)
        far_copies.append(send(offset_pair.at[:, there], far_offset.at[:, z], far_peer(there)))
    own = pltpu.make_async_copy(offset_pair.at[:, z], far_offset.at[:, z], local_sem.at[1])
    own.start()

    def ready(k):
        for number, step in zip(lines_sent[k], (2, 1, 3)):
            source = lax.rem(x + 4 - step, 4)
            arrive(number, block(core, source, targets[k]), {"vocab_2": source})
            to_core(k, source)
        for number, which_x in shares[k]:
            arrive(number, block(1 - core, which_x, targets[k]), other_core)

    def multiply(slot, target):
        at = pl.ds(pl.multiple_of(target * strip, strip), strip)
        for k in range(PARTS):
            cut = pl.ds(k * wide, wide)
            total = jnp.dot(
                hidden[0, :, at, :].reshape(rows, half),
                weights[:half, cut],
                preferred_element_type=jnp.float32,
            ) + jnp.dot(
                hidden[1, :, at, :].reshape(rows, half),
                weights[half:, cut],
                preferred_element_type=jnp.float32,
            )
            for i in range(4):
                for j in range(4):
                    partial[slot, pl.ds((j * 4 + i) * 8, 8), cut] = total[
                        (i * 4 + j) * 8 : (i * 4 + j + 1) * 8
                    ]

    first, last = pl.ds(0, mid), pl.ds(mid, mid)
    def turn(tile):
        return tile.T[0:1, :]

    def spread(line):
        return jnp.broadcast_to(line, (128, rows)).T

    def peak(slot):
        most = jnp.abs(partial[slot, :, pl.ds(0, 128)])
        for k in range(1, columns // 128):
            most = jnp.maximum(most, jnp.abs(partial[slot, :, pl.ds(k * 128, 128)]))
        most = jnp.maximum(jnp.max(most, axis=1, keepdims=True), 1e-30)
        return jnp.broadcast_to(most, (rows, 128))

    def encode(box, cut, value, gain):
        gain = jnp.concatenate([gain] * (value.shape[1] // 128), axis=1)
        whole = jnp.round(value * gain).astype(jnp.int32)
        coded[box, pl.ds(0, mid), cut] = (whole >> 4).astype(jnp.int16)
        low = whole & 15
        packed = low[:quarter]
        for k in range(1, 4):
            packed = packed | (low[k * quarter : (k + 1) * quarter] << (4 * k))
        coded[box, pl.ds(mid, quarter), cut] = (packed - 32768).astype(jnp.int16)
        return coded.at[box, :, cut]

    def decode(box, cut, unit):
        high = box[pl.ds(0, mid), cut].astype(jnp.int32)
        packed = box[pl.ds(mid, quarter), cut].astype(jnp.int32) + 32768
        low = jnp.concatenate([(packed >> (4 * k)) & 15 for k in range(4)])
        value = ((high << 4) + low).astype(jnp.float32)
        return value * jnp.concatenate([unit] * (value.shape[1] // 128), axis=1)

    quarter = mid // 4
    cuts = [pl.ds(k * wide, wide) for k in range(PARTS)]
    relays = []
    ready(0)
    load.wait()
    multiply(0, targets[0])
    peak_0 = peak(0)
    gain = LIMIT / peak_0
    scale_out[0] = turn(peak_0)
    scale_up = send(scale_out.at[0], scale_in.at[0], after)
    scale_down = send(scale_out.at[0], scale_in.at[1], before)
    for cut in cuts:
        one = encode(0, cut, partial[0, first, cut], gain[:mid])
        one = send(one, relay_in.at[0, :, cut], after)
        two = encode(1, cut, partial[0, last, cut], gain[mid:])
        relays.append((one, send(two, relay_in.at[1, :, cut], before)))
    ready(1)
    multiply(1, targets[1])
    peak_1 = peak(1)
    gain = LIMIT / peak_1
    directs = []
    for cut in cuts:
        one = encode(2, cut, partial[1, last, cut], gain[mid:])
        directs.append([send(one, direct_in.at[0, :, cut], after)])
    ready(2)
    multiply(2, targets[2])
    peak_2 = peak(2)
    gain = LIMIT / peak_2
    for k, cut in enumerate(cuts):
        two = encode(3, cut, partial[2, first, cut], gain[:mid])
        directs[k].append(send(two, direct_in.at[1, :, cut], before))

    arrive(scale_up, scale_in.at[0], before)
    arrive(scale_down, scale_in.at[1], after)
    peak_up, peak_down = spread(scale_in[0])[:mid], spread(scale_in[1])[mid:]
    bound_up, bound_down = peak_up + peak_1[:mid], peak_down + peak_2[mid:]
    scale_out[1] = turn(jnp.concatenate([bound_up, peak_1[mid:]]))
    scale_out[2] = turn(jnp.concatenate([peak_2[:mid], bound_down]))
    scale_up = send(scale_out.at[1], scale_in.at[2], after)
    scale_down = send(scale_out.at[2], scale_in.at[3], before)

    own.wait()
    for step in range(1, FAR):
        source = lax.rem(z + FAR - step, FAR)
        arrive(far_copies[step - 1], far_offset.at[:, source], far_peer(source))
    pair_copies = []
    for step in range(1, 8):
        there = lax.rem(pair + step, 8)
        pair_copies.append(
            send(far_offset.at[:, :, there], near_offset.at[:, :, pair], pair_peer(there))
        )
    own = pltpu.make_async_copy(
        far_offset.at[:, :, pair], near_offset.at[:, :, pair], local_sem.at[2]
    )
    own.start()

    finals = []
    gain_up, gain_down = LIMIT / bound_up, LIMIT / bound_down
    unit_up, unit_down = peak_up * (1.0 / LIMIT), peak_down * (1.0 / LIMIT)
    for k, cut in enumerate(cuts):
        arrive(relays[k][0], relay_in.at[0, :, cut], before)
        value = partial[1, first, cut] + decode(relay_in.at[0], cut, unit_up)
        one = send(encode(4, cut, value, gain_up), final_in.at[0, :, cut], after)
        arrive(relays[k][1], relay_in.at[1, :, cut], after)
        value = partial[2, last, cut] + decode(relay_in.at[1], cut, unit_down)
        two = send(encode(5, cut, value, gain_down), final_in.at[1, :, cut], before)
        finals.append((one, two))
    ready(3)
    multiply(3, targets[3])

    own.wait()
    for step in range(1, 8):
        source = lax.rem(pair + 8 - step, 8)
        arrive(pair_copies[step - 1], near_offset.at[:, :, source], pair_peer(source))
    offset[...] = near_offset[...].astype(jnp.float32)

    factor = spread(divisor[...])
    inverse = 1.0 / factor
    cooler = 1.0 / spread(softening[...])
    arrive(scale_up, scale_in.at[2], before)
    arrive(scale_down, scale_in.at[3], after)
    unit_up = spread(scale_in[2]) * (1.0 / LIMIT)
    unit_down = spread(scale_in[3]) * (1.0 / LIMIT)
    highest = None
    for k, cut in enumerate(cuts):
        arrive(directs[k][0], direct_in.at[0, :, cut], before)
        arrive(directs[k][1], direct_in.at[1, :, cut], after)
        arrive(finals[k][0], final_in.at[0, :, cut], before)
        arrive(finals[k][1], final_in.at[1, :, cut], after)
        for j in range(k * wide // 128, (k + 1) * wide // 128):
            at = pl.ds(j * 128, 128)
            upper = partial[3, first, at] + (
                decode(final_in.at[0], at, unit_up[:mid])
                + decode(direct_in.at[1], at, unit_down[:mid])
            )
            lower = partial[3, last, at] + (
                decode(final_in.at[1], at, unit_down[mid:])
                + decode(direct_in.at[0], at, unit_up[mid:])
            )
            raw = jnp.concatenate([upper, lower])
            shift = offset[:, :, :, j, :].reshape(rows, 128)
            scaled = jnp.where(raw > 0, raw * inverse, raw * factor)
            changed = jnp.where(shift < 0, scaled, raw) + shift
            changed_out[:, at] = changed.astype(jnp.bfloat16)
            turned = (changed * cooler).T
            scores[at, :] = turned
            most = jnp.max(turned, axis=0, keepdims=True)
            highest = most if highest is None else jnp.maximum(highest, most)

    def sems(turn):
        return (
            sem_near_send.at[turn],
            sem_near_recv.at[turn],
            sem_far_send.at[turn],
            sem_far_recv.at[turn],
        )

    leave = pltpu.make_async_copy(changed_out, out, local_sem.at[3])
    leave.start()
    largest, more = reduced(highest, near_a, far_a, sems(0), jnp.maximum)
    sent += more
    total = jnp.zeros((8, 128), jnp.float32)
    chunk = 64
    for k in range(scores.shape[0] // chunk):
        at = pl.ds(k * chunk, chunk)
        grown = jnp.exp(scores[at, :] - largest)
        terms[at, :] = grown
        total = total + jnp.sum(grown.reshape(chunk // 8, 8, 128), axis=0)

    first = [largest - (SPAN / (LEVELS[0] + 1)) * (k + 1) for k in range(LEVELS[0])]
    rows = [jnp.sum(total, axis=0, keepdims=True)] + masses(scores, terms, first)
    sums, more = reduced(jnp.concatenate(rows), near_b, far_b, sems(1), jnp.add)
    sent += more
    target = share[...] * sums[0:1]
    lower = jnp.sum(
        jnp.where(sums[1:] < target, 1.0, 0.0), axis=0, keepdims=True
    ) * (LEVELS[1] + 1)

    unit = SPAN / ((LEVELS[0] + 1) * (LEVELS[1] + 1))
    second = [largest - unit * (lower + (k + 1)) for k in range(LEVELS[1])]
    rows = masses(scores, terms, second)
    rows.append(rows[-1])
    sums, more = reduced(jnp.concatenate(rows), near_c, far_c, sems(2), jnp.add)
    sent += more
    below = jnp.where(sums[: LEVELS[1]] < target, 1.0, 0.0)
    lower = lower + jnp.sum(below, axis=0, keepdims=True)
    cutoff[...] = largest - unit * (lower + 1.0)
    leave.wait()
    for copy in sent:
        copy.wait_send()


def settle_kernel(out, cutoff, out_kept, cutoff_kept):
    out_kept[...] = out[...]
    cutoff_kept[...] = cutoff[...]


def step(latent, weights, tally, table, charge, appearance, *by_row):
    depth, columns = weights.shape
    rows = by_row[0].shape[0]
    vmem = pl.BlockSpec(memory_space=pltpu.VMEM)

    def held(count, lines):
        return pltpu.VMEM((count, lines, 128), jnp.float32)

    def whole(*shape):
        return pltpu.VMEM(shape, jnp.float32)

    def boxes(count):
        return pltpu.VMEM((count, rows * 5 // 8, columns), jnp.int16)

    results = (
        jax.ShapeDtypeStruct((rows, columns), jnp.bfloat16),
        jax.ShapeDtypeStruct((1, rows), jnp.float32),
    )
    found = pl.pallas_call(
        step_kernel,
        out_shape=results,
        in_specs=[vmem, pl.BlockSpec(memory_space=pl.ANY)] + [vmem] * 7,
        out_specs=(pl.BlockSpec(memory_space=pl.ANY), vmem),
        scratch_shapes=[
            pltpu.VMEM((depth, columns), weights.dtype),
            whole(2, FAR, 8, columns // 128, 128),
            pltpu.VMEM((GROUP, latent.shape[0], depth // 2), latent.dtype),
            pltpu.VMEM((2, 4, rows, depth // 2), latent.dtype),
            whole(4, rows, columns),
            boxes(6),
            boxes(2),
            boxes(2),
            boxes(2),
            whole(3, 1, 128),
            whole(4, 1, 128),
            pltpu.VMEM((FAR, 8, columns // 128, 128), jnp.bfloat16),
            pltpu.VMEM((2, FAR, 8, columns // 128, 128), jnp.bfloat16),
            pltpu.VMEM((2, FAR, 8, columns // 128, 128), jnp.bfloat16),
            pltpu.VMEM((2, FAR, 8, columns // 128, 128), jnp.bfloat16),
            pltpu.VMEM((rows, columns), jnp.bfloat16),
            whole(columns, rows),
            whole(columns, rows),
            held(NEAR, 1),
            held(FAR, 1),
            held(NEAR, LEVELS[0] + 1),
            held(FAR, LEVELS[0] + 1),
            held(NEAR, LEVELS[1] + 1),
            held(FAR, LEVELS[1] + 1),
            pltpu.SemaphoreType.DMA((COPIES,)),
            pltpu.SemaphoreType.DMA((COPIES,)),
            pltpu.SemaphoreType.DMA((4,)),
            pltpu.SemaphoreType.DMA((3, NEAR)),
            pltpu.SemaphoreType.DMA((3, NEAR)),
            pltpu.SemaphoreType.DMA((3, FAR)),
            pltpu.SemaphoreType.DMA((3, FAR)),
        ],
        compiler_params=pltpu.CompilerParams(
            collective_id=1, has_side_effects=True, vmem_limit_bytes=56 * 2**20
        ),
        name="step",
    )(
        latent,
        weights,
        tally.reshape(-1, 128),
        table,
        charge[None, :],
        appearance[None, :],
        *(part[None, :] for part in by_row),
    )
    return pl.pallas_call(
        settle_kernel,
        out_shape=results,
        in_specs=[vmem, vmem],
        out_specs=(vmem, vmem),
        name="settle",
    )(*found)


def per_device(*arguments):
    out, cutoff = step(*arguments)
    return out, cutoff.reshape(-1)


def solution(mesh):
    split = Mesh(
        mesh.devices.reshape(2, 8, 4, 2, mesh.shape["seq"]),
        ("vocab_0", "vocab_1", "vocab_2", "vocab_3", "seq"),
    )
    placed = (
        P(VOCAB, "seq"),
        P("seq", VOCAB),
        P(SEQ_VOCAB, None),
        P(SEQ_VOCAB, None),
        P(SEQ_VOCAB),
        P(SEQ_VOCAB),
        P("seq"),
        P("seq"),
        P("seq"),
    )
    return jax.shard_map(
        per_device,
        mesh=split,
        in_specs=placed,
        out_specs=(P("seq", VOCAB), P("seq")),
        check_vma=False,
    )
```

```python
import functools
import itertools

import jax
import jax.numpy as jnp
from jax import lax
from jax.experimental import pallas as pl
from jax.experimental.pallas import tpu as pltpu
from jax.sharding import Mesh
from jax.sharding import PartitionSpec as P

VOCAB = ("vocab_0", "vocab_1", "vocab_2", "vocab_3")
SEQ_VOCAB = ("seq", "vocab_0", "vocab_1", "vocab_2", "vocab_3")
MESH = pl.DeviceIdType.MESH
NEAR = 16
FAR = 8
LEVELS = (31, 15)
SPLIT = (2, 2)
SPAN = 32.0
PARTS = 4
GROUP = 32
COPIES = 112
LIMIT = 524280.0


def near_index():
    return (
        lax.axis_index("vocab_0") * 8
        + lax.axis_index("vocab_2") * 2
        + lax.axis_index("vocab_3")
    )


def near_peer(index):
    return {
        "vocab_0": index // 8,
        "vocab_2": lax.rem(index // 2, 4),
        "vocab_3": lax.rem(index, 2),
    }


def group_peer(index):
    return {
        "vocab_0": index // 16,
        "vocab_1": lax.rem(index // 2, 8),
        "vocab_3": lax.rem(index, 2),
    }


def pair_peer(index):
    return {"vocab_2": index // 2, "vocab_3": lax.rem(index, 2)}


def far_peer(index):
    return {"vocab_1": index}


def near_distance(step):
    return (step // 8) + min(step // 2 % 4, 4 - step // 2 % 4)


def far_distance(step):
    return min(step, FAR - step)


def begin(held, me, count, peer, distance, send_sem, recv_sem):
    copies = []
    for step in sorted(range(1, count), key=lambda k: -distance(k)):
        copy = pltpu.make_async_remote_copy(
            src_ref=held.at[me],
            dst_ref=held.at[me],
            send_sem=send_sem.at[step],
            recv_sem=recv_sem.at[step],
            device_id=peer(lax.rem(me + step, count)),
            device_id_type=MESH,
        )
        copy.start()
        copies.append(copy)
    return copies


def finish(held, me, count, peer, distance, send_sem, recv_sem, combine):
    for step in range(1, count):
        source = lax.rem(me + count - step, count)
        pltpu.make_async_remote_copy(
            src_ref=held.at[me],
            dst_ref=held.at[source],
            send_sem=send_sem.at[step],
            recv_sem=recv_sem.at[step],
            device_id=peer(source),
            device_id_type=MESH,
        ).wait_recv()
    whole = held[0]
    for k in range(1, count):
        whole = combine(whole, held[k])
    return whole


def reduced(parts, near, far, sems, combine):
    here, there = near_index(), lax.axis_index("vocab_1")
    sent, wholes = [], []
    ways = [
        (
            (near.at[k], here, NEAR, near_peer, near_distance, sems[0].at[k], sems[1].at[k]),
            (far.at[k], there, FAR, far_peer, far_distance, sems[2].at[k], sems[3].at[k]),
        )
        for k in range(len(parts))
    ]
    for k, part in enumerate(parts):
        near[k, here] = part()
        sent += begin(*ways[k][0])
    for k in range(len(parts)):
        far[k, there] = finish(*ways[k][0], combine)
        sent += begin(*ways[k][1])
    for k in range(len(parts)):
        wholes.append(finish(*ways[k][1], combine))
    return jnp.concatenate(wholes), sent


def masses(scores, weights, limits):
    rows = []
    chunks = scores.shape[0] // 8
    for start in range(0, len(limits), 8):
        group = [jnp.broadcast_to(t, (8, 128)) for t in limits[start : start + 8]]

        def add(k, sums, group=group):
            at = pl.ds(pl.multiple_of(k * 8, 8), 8)
            s, w = scores[at, :], weights[at, :]
            return tuple(a + jnp.where(s >= t, w, 0.0) for a, t in zip(sums, group))

        zero = jnp.zeros((8, 128), jnp.float32)
        sums = lax.fori_loop(0, chunks, add, (zero,) * len(group), unroll=8)
        rows += [jnp.sum(a, axis=0, keepdims=True) for a in sums]
    return rows


def step_kernel(
    latent,
    weights_hbm,
    tally,
    table,
    charge,
    appearance,
    divisor,
    softening,
    share,
    out,
    cutoff,
    weights,
    offset,
    few,
    hidden,
    partial,
    coded,
    relay_in,
    direct_in,
    final_in,
    scale_out,
    scale_in,
    offset_out,
    offset_pair,
    far_offset,
    near_offset,
    changed_out,
    scores,
    terms,
    near_a,
    far_a,
    near_b,
    far_b,
    near_c,
    far_c,
    send_sem,
    recv_sem,
    local_sem,
    *round_sems,
):
    y, z = lax.axis_index("vocab_0"), lax.axis_index("vocab_1")
    x, core = lax.axis_index("vocab_2"), lax.axis_index("vocab_3")
    seq = lax.axis_index("seq")
    here, pair = near_index(), x * 2 + core
    half = latent.shape[1] // 2
    rows, columns = out.shape
    mid, wide = rows // 2, columns // PARTS

    load = pltpu.make_async_copy(weights_hbm, weights, local_sem.at[0])
    load.start()
    barrier = pltpu.get_barrier_semaphore()

    def greet(peer):
        pl.semaphore_signal(barrier, inc=1, device_id=peer, device_id_type=MESH)

    group = (y * FAR + z) * 2 + core
    for step in range(1, GROUP):
        greet(group_peer(lax.rem(group + step, GROUP)))
    for step in range(1, NEAR):
        greet(near_peer(lax.rem(here + step, NEAR)))
    after, before = {"seq": lax.rem(seq + 1, 4)}, {"seq": lax.rem(seq + 3, 4)}
    greet(after)
    greet(before)

    numbers = itertools.count()
    sent = []

    def describe(number, source, target, peer):
        return pltpu.make_async_remote_copy(
            src_ref=source,
            dst_ref=target,
            send_sem=send_sem.at[number],
            recv_sem=recv_sem.at[number],
            device_id=peer,
            device_id_type=MESH,
        )

    def send(source, target, peer):
        number = next(numbers)
        copy = describe(number, source, target, peer)
        copy.start()
        sent.append(copy)
        return number

    def arrive(number, landing, peer):
        describe(number, landing, landing, peer).wait_recv()

    def my_half(which):
        return pl.ds(pl.multiple_of(which * half, 128), half)

    few[group] = latent[:, my_half(core)]
    pl.semaphore_wait(barrier, NEAR + GROUP)

    swaps = {}
    for step in sorted(range(1, GROUP), key=lambda k: -min(k // 2 % 8, 8 - k // 2 % 8)):
        there = lax.rem(group + step, GROUP)
        swaps[step] = send(
            latent.at[:, my_half(lax.rem(there, 2))], few.at[group], group_peer(there)
        )

    flat = offset.reshape(tally.shape[0], 128)
    lines = 64
    each = jnp.broadcast_to(charge[...], (lines, 128))
    once = jnp.broadcast_to(appearance[...], (lines, 128))

    def shift_lines(k, carry):
        base = pl.multiple_of(k * lines, lines)
        line = table[:, pl.ds(pl.multiple_of(base * 128, lines * 128), lines * 128)]
        line = line.astype(jnp.float32)
        for j in range(lines):
            flat[pl.ds(base + j, 1), :] = line[:, j * 128 : (j + 1) * 128]
        at = pl.ds(base, lines)
        count = tally[at, :].astype(jnp.float32)
        value = (
            flat[at, :] - each * count - once * jnp.where(count > 0, 1.0, 0.0)
        )
        flat[at, :] = value
        return carry

    lax.fori_loop(0, tally.shape[0] // lines, shift_lines, 0)
    other_y = {"vocab_0": 1 - y}
    offset_out[...] = offset[1 - y].astype(jnp.bfloat16)
    offset_pair[y] = offset[y].astype(jnp.bfloat16)
    crossing = send(offset_out, offset_pair.at[y], other_y)

    for step in range(1, GROUP):
        source = lax.rem(group + GROUP - step, GROUP)
        arrive(swaps[step], few.at[source], group_peer(source))

    other_core = {"vocab_3": 1 - core}
    strip = rows // 4
    targets = [lax.rem(seq + k, 4) for k in (2, 1, 3, 0)]

    def block(side, which_x, target):
        at = pl.multiple_of(target * strip, strip)
        return hidden.at[side, which_x, pl.ds(at, strip)]

    for k in range(4):
        joined = [few[k * 8 + j].astype(jnp.float32) for j in range(8)]
        hidden[core, x, pl.ds(k * strip, strip)] = jnp.concatenate(joined).astype(jnp.bfloat16)

    shares, lines_sent = [[] for _ in targets], []

    def to_core(k, which_x):
        piece = block(core, which_x, targets[k])
        shares[k].append((send(piece, piece, other_core), which_x))

    for k, target in enumerate(targets):
        piece = block(core, x, target)
        lines_sent.append(
            [
                send(piece, piece, {"vocab_2": lax.rem(x + step, 4)})
                for step in (2, 1, 3)
            ]
        )
        to_core(k, x)

    arrive(crossing, offset_pair.at[1 - y], other_y)
    far_copies = []
    for step in range(1, FAR):
        there = lax.rem(z + step, FAR)
        far_copies.append(send(offset_pair.at[:, there], far_offset.at[:, z], far_peer(there)))
    own = pltpu.make_async_copy(offset_pair.at[:, z], far_offset.at[:, z], local_sem.at[1])
    own.start()

    def ready(k):
        for number, step in zip(lines_sent[k], (2, 1, 3)):
            source = lax.rem(x + 4 - step, 4)
            arrive(number, block(core, source, targets[k]), {"vocab_2": source})
            to_core(k, source)
        for number, which_x in shares[k]:
            arrive(number, block(1 - core, which_x, targets[k]), other_core)

    def multiply(slot, target):
        at = pl.ds(pl.multiple_of(target * strip, strip), strip)
        for k in range(PARTS):
            cut = pl.ds(k * wide, wide)
            total = jnp.dot(
                hidden[0, :, at, :].reshape(rows, half),
                weights[:half, cut],
                preferred_element_type=jnp.float32,
            ) + jnp.dot(
                hidden[1, :, at, :].reshape(rows, half),
                weights[half:, cut],
                preferred_element_type=jnp.float32,
            )
            for i in range(4):
                for j in range(4):
                    partial[slot, pl.ds((j * 4 + i) * 8, 8), cut] = total[
                        (i * 4 + j) * 8 : (i * 4 + j + 1) * 8
                    ]

    first, last = pl.ds(0, mid), pl.ds(mid, mid)
    def turn(tile):
        return tile.T[0:1, :]

    def spread(line):
        return jnp.broadcast_to(line, (128, rows)).T

    def peak(slot):
        most = jnp.abs(partial[slot, :, pl.ds(0, 128)])
        for k in range(1, columns // 128):
            most = jnp.maximum(most, jnp.abs(partial[slot, :, pl.ds(k * 128, 128)]))
        most = jnp.maximum(jnp.max(most, axis=1, keepdims=True), 1e-30)
        return jnp.broadcast_to(most, (rows, 128))

    def encode(box, cut, value, gain):
        gain = jnp.concatenate([gain] * (value.shape[1] // 128), axis=1)
        whole = jnp.round(value * gain).astype(jnp.int32)
        coded[box, pl.ds(0, mid), cut] = (whole >> 4).astype(jnp.int16)
        low = whole & 15
        packed = low[:quarter]
        for k in range(1, 4):
            packed = packed | (low[k * quarter : (k + 1) * quarter] << (4 * k))
        coded[box, pl.ds(mid, quarter), cut] = (packed - 32768).astype(jnp.int16)
        return coded.at[box, :, cut]

    def decode(box, cut, unit):
        high = box[pl.ds(0, mid), cut].astype(jnp.int32)
        packed = box[pl.ds(mid, quarter), cut].astype(jnp.int32) + 32768
        low = jnp.concatenate([(packed >> (4 * k)) & 15 for k in range(4)])
        value = ((high << 4) + low).astype(jnp.float32)
        return value * jnp.concatenate([unit] * (value.shape[1] // 128), axis=1)

    quarter = mid // 4
    cuts = [pl.ds(k * wide, wide) for k in range(PARTS)]
    relays = []
    ready(0)
    load.wait()
    multiply(0, targets[0])
    peak_0 = peak(0)
    gain = LIMIT / peak_0
    scale_out[0] = turn(peak_0)
    scale_up = send(scale_out.at[0], scale_in.at[0], after)
    scale_down = send(scale_out.at[0], scale_in.at[1], before)
    for cut in cuts:
        one = encode(0, cut, partial[0, first, cut], gain[:mid])
        one = send(one, relay_in.at[0, :, cut], after)
        two = encode(1, cut, partial[0, last, cut], gain[mid:])
        relays.append((one, send(two, relay_in.at[1, :, cut], before)))
    ready(1)
    multiply(1, targets[1])
    peak_1 = peak(1)
    gain = LIMIT / peak_1
    directs = []
    for cut in cuts:
        one = encode(2, cut, partial[1, last, cut], gain[mid:])
        directs.append([send(one, direct_in.at[0, :, cut], after)])
    ready(2)
    multiply(2, targets[2])
    peak_2 = peak(2)
    gain = LIMIT / peak_2
    for k, cut in enumerate(cuts):
        two = encode(3, cut, partial[2, first, cut], gain[:mid])
        directs[k].append(send(two, direct_in.at[1, :, cut], before))

    arrive(scale_up, scale_in.at[0], before)
    arrive(scale_down, scale_in.at[1], after)
    peak_up, peak_down = spread(scale_in[0])[:mid], spread(scale_in[1])[mid:]
    bound_up, bound_down = peak_up + peak_1[:mid], peak_down + peak_2[mid:]
    scale_out[1] = turn(jnp.concatenate([bound_up, peak_1[mid:]]))
    scale_out[2] = turn(jnp.concatenate([peak_2[:mid], bound_down]))
    scale_up = send(scale_out.at[1], scale_in.at[2], after)
    scale_down = send(scale_out.at[2], scale_in.at[3], before)

    own.wait()
    for step in range(1, FAR):
        source = lax.rem(z + FAR - step, FAR)
        arrive(far_copies[step - 1], far_offset.at[:, source], far_peer(source))
    pair_copies = []
    for step in range(1, 8):
        there = lax.rem(pair + step, 8)
        pair_copies.append(
            send(far_offset.at[:, :, there], near_offset.at[:, :, pair], pair_peer(there))
        )
    own = pltpu.make_async_copy(
        far_offset.at[:, :, pair], near_offset.at[:, :, pair], local_sem.at[2]
    )
    own.start()

    finals = []
    gain_up, gain_down = LIMIT / bound_up, LIMIT / bound_down
    unit_up, unit_down = peak_up * (1.0 / LIMIT), peak_down * (1.0 / LIMIT)
    for k, cut in enumerate(cuts):
        arrive(relays[k][0], relay_in.at[0, :, cut], before)
        value = partial[1, first, cut] + decode(relay_in.at[0], cut, unit_up)
        one = send(encode(4, cut, value, gain_up), final_in.at[0, :, cut], after)
        arrive(relays[k][1], relay_in.at[1, :, cut], after)
        value = partial[2, last, cut] + decode(relay_in.at[1], cut, unit_down)
        two = send(encode(5, cut, value, gain_down), final_in.at[1, :, cut], before)
        finals.append((one, two))
    ready(3)
    multiply(3, targets[3])

    own.wait()
    for step in range(1, 8):
        source = lax.rem(pair + 8 - step, 8)
        arrive(pair_copies[step - 1], near_offset.at[:, :, source], pair_peer(source))
    offset[...] = near_offset[...].astype(jnp.float32)

    factor = spread(divisor[...])
    inverse = 1.0 / factor
    cooler = 1.0 / spread(softening[...])
    arrive(scale_up, scale_in.at[2], before)
    arrive(scale_down, scale_in.at[3], after)
    unit_up = spread(scale_in[2]) * (1.0 / LIMIT)
    unit_down = spread(scale_in[3]) * (1.0 / LIMIT)
    highest = None
    for k, cut in enumerate(cuts):
        arrive(directs[k][0], direct_in.at[0, :, cut], before)
        arrive(directs[k][1], direct_in.at[1, :, cut], after)
        arrive(finals[k][0], final_in.at[0, :, cut], before)
        arrive(finals[k][1], final_in.at[1, :, cut], after)
        for j in range(k * wide // 128, (k + 1) * wide // 128):
            at = pl.ds(j * 128, 128)
            upper = partial[3, first, at] + (
                decode(final_in.at[0], at, unit_up[:mid])
                + decode(direct_in.at[1], at, unit_down[:mid])
            )
            lower = partial[3, last, at] + (
                decode(final_in.at[1], at, unit_down[mid:])
                + decode(direct_in.at[0], at, unit_up[mid:])
            )
            raw = jnp.concatenate([upper, lower])
            shift = offset[:, :, :, j, :].reshape(rows, 128)
            scaled = jnp.where(raw > 0, raw * inverse, raw * factor)
            changed = jnp.where(shift < 0, scaled, raw) + shift
            changed_out[:, at] = changed.astype(jnp.bfloat16)
            turned = (changed * cooler).T
            scores[at, :] = turned
            most = jnp.max(turned, axis=0, keepdims=True)
            highest = most if highest is None else jnp.maximum(highest, most)

    sems = [round_sems[4 * k : 4 * k + 4] for k in range(3)]
    leave = pltpu.make_async_copy(changed_out, out, local_sem.at[3])
    leave.start()
    largest, more = reduced([lambda: highest], near_a, far_a, sems[0], jnp.maximum)
    sent += more
    total = jnp.zeros((8, 128), jnp.float32)
    chunk = 64
    for k in range(scores.shape[0] // chunk):
        at = pl.ds(k * chunk, chunk)
        grown = jnp.exp(scores[at, :] - largest)
        terms[at, :] = grown
        total = total + jnp.sum(grown.reshape(chunk // 8, 8, 128), axis=0)

    first = [largest - (SPAN / (LEVELS[0] + 1)) * (k + 1) for k in range(LEVELS[0])]
    total = jnp.sum(total, axis=0, keepdims=True)

    def cut_masses(limits, lead=None):
        found = masses(scores, terms, limits)
        return jnp.concatenate(found if lead is None else [lead] + found)

    depth = (LEVELS[0] + 1) // SPLIT[0]
    parts = [functools.partial(cut_masses, first[: depth - 1], total)]
    for k in range(1, SPLIT[0]):
        parts.append(functools.partial(cut_masses, first[k * depth - 1 : (k + 1) * depth - 1]))
    sums, more = reduced(parts, near_b, far_b, sems[1], jnp.add)
    sent += more
    target = share[...] * sums[0:1]
    lower = jnp.sum(
        jnp.where(sums[1:] < target, 1.0, 0.0), axis=0, keepdims=True
    ) * (LEVELS[1] + 1)

    unit = SPAN / ((LEVELS[0] + 1) * (LEVELS[1] + 1))
    second = [largest - unit * (lower + (k + 1)) for k in range(LEVELS[1])]
    depth = (LEVELS[1] + 1) // SPLIT[1]
    second.append(second[-1])
    parts = [
        functools.partial(cut_masses, second[k * depth : (k + 1) * depth])
        for k in range(SPLIT[1])
    ]
    sums, more = reduced(parts, near_c, far_c, sems[2], jnp.add)
    sent += more
    below = jnp.where(sums[: LEVELS[1]] < target, 1.0, 0.0)
    lower = lower + jnp.sum(below, axis=0, keepdims=True)
    cutoff[...] = largest - unit * (lower + 1.0)
    leave.wait()
    for copy in sent:
        copy.wait_send()


def settle_kernel(out, cutoff, out_kept, cutoff_kept):
    out_kept[...] = out[...]
    cutoff_kept[...] = cutoff[...]


def step(latent, weights, tally, table, charge, appearance, *by_row):
    depth, columns = weights.shape
    rows = by_row[0].shape[0]
    vmem = pl.BlockSpec(memory_space=pltpu.VMEM)

    def held(split, count, lines):
        return pltpu.VMEM((split, count, lines, 128), jnp.float32)

    def whole(*shape):
        return pltpu.VMEM(shape, jnp.float32)

    def boxes(count):
        return pltpu.VMEM((count, rows * 5 // 8, columns), jnp.int16)

    results = (
        jax.ShapeDtypeStruct((rows, columns), jnp.bfloat16),
        jax.ShapeDtypeStruct((1, rows), jnp.float32),
    )
    found = pl.pallas_call(
        step_kernel,
        out_shape=results,
        in_specs=[vmem, pl.BlockSpec(memory_space=pl.ANY)] + [vmem] * 7,
        out_specs=(pl.BlockSpec(memory_space=pl.ANY), vmem),
        scratch_shapes=[
            pltpu.VMEM((depth, columns), weights.dtype),
            whole(2, FAR, 8, columns // 128, 128),
            pltpu.VMEM((GROUP, latent.shape[0], depth // 2), latent.dtype),
            pltpu.VMEM((2, 4, rows, depth // 2), latent.dtype),
            whole(4, rows, columns),
            boxes(6),
            boxes(2),
            boxes(2),
            boxes(2),
            whole(3, 1, 128),
            whole(4, 1, 128),
            pltpu.VMEM((FAR, 8, columns // 128, 128), jnp.bfloat16),
            pltpu.VMEM((2, FAR, 8, columns // 128, 128), jnp.bfloat16),
            pltpu.VMEM((2, FAR, 8, columns // 128, 128), jnp.bfloat16),
            pltpu.VMEM((2, FAR, 8, columns // 128, 128), jnp.bfloat16),
            pltpu.VMEM((rows, columns), jnp.bfloat16),
            whole(columns, rows),
            whole(columns, rows),
            held(1, NEAR, 1),
            held(1, FAR, 1),
            held(SPLIT[0], NEAR, (LEVELS[0] + 1) // SPLIT[0]),
            held(SPLIT[0], FAR, (LEVELS[0] + 1) // SPLIT[0]),
            held(SPLIT[1], NEAR, (LEVELS[1] + 1) // SPLIT[1]),
            held(SPLIT[1], FAR, (LEVELS[1] + 1) // SPLIT[1]),
            pltpu.SemaphoreType.DMA((COPIES,)),
            pltpu.SemaphoreType.DMA((COPIES,)),
            pltpu.SemaphoreType.DMA((4,)),
        ]
        + [
            pltpu.SemaphoreType.DMA((split, count))
            for split in (1, *SPLIT)
            for count in (NEAR, NEAR, FAR, FAR)
        ],
        compiler_params=pltpu.CompilerParams(
            collective_id=1, has_side_effects=True, vmem_limit_bytes=56 * 2**20
        ),
        name="step",
    )(
        latent,
        weights,
        tally.reshape(-1, 128),
        table,
        charge[None, :],
        appearance[None, :],
        *(part[None, :] for part in by_row),
    )
    return pl.pallas_call(
        settle_kernel,
        out_shape=results,
        in_specs=[vmem, vmem],
        out_specs=(vmem, vmem),
        name="settle",
    )(*found)


def per_device(*arguments):
    out, cutoff = step(*arguments)
    return out, cutoff.reshape(-1)


def solution(mesh):
    split = Mesh(
        mesh.devices.reshape(2, 8, 4, 2, mesh.shape["seq"]),
        ("vocab_0", "vocab_1", "vocab_2", "vocab_3", "seq"),
    )
    placed = (
        P(VOCAB, "seq"),
        P("seq", VOCAB),
        P(SEQ_VOCAB, None),
        P(SEQ_VOCAB, None),
        P(SEQ_VOCAB),
        P(SEQ_VOCAB),
        P("seq"),
        P("seq"),
        P("seq"),
    )
    return jax.shard_map(
        per_device,
        mesh=split,
        in_specs=placed,
        out_specs=(P("seq", VOCAB), P("seq")),
        check_vma=False,
    )
```
